128 devices in a mesh: row: 16 (over x, z), col: 8 (over y, core).
Axes of the slice: x: 4, y: 4, z: 4, core: 2. Of those that a mesh axis runs over, the one named last changes fastest.
Arguments:
- prior_covariance: float32 [16384, 16384], P('row', 'col'), may hold values from -1 to 12, as said below
- vel_first: float32 [128, 128], replicated, may hold values from -0.25 to 0.25
- vel_second: float32 [128, 128], replicated, may hold values from -0.25 to 0.25
- obs_cell: int32 [512, 2], replicated, may hold values from 0 to 126, as said below
- obs_noise: float32 [512], replicated, may hold values from 0.1 to 1
Outputs:
- analysis_covariance: float32 [16384, 16384], P('row', 'col')
The draws below stay inside these ranges and needn't reach their ends.
Inputs may be any that keep to these rules, and one draw needn't show every extreme that they name: `prior_covariance`: symmetric and positive definite. Observation o interpolates the cells (i, j), (i, j + 1), (i + 1, j), (i + 1, j + 1) with i = obs_cell[o, 0] and j = obs_cell[o, 1].
All inputs are finite; a program needn't handle non-finite values.
Results may differ from the reference program's by a relative error of at most 0.000065.
Values sent between devices are 32-bit elements; how exact they have to be, the bound alone decides.
A program may use at most 192 MiB of HBM per device.

```python
import math
import jax
import jax.numpy as jnp
from jax import lax

GRID = 128
MEASURE_TOTAL = 512
SYSTEM_ORDER = 16384


def draw_prior_covariance(key, part):
    state_order = GRID * GRID
    base_key, diag_key = jax.random.split(jax.random.fold_in(key, 7), 2)
    spread = 1.5 / GRID
    uniform_part = jax.random.uniform(base_key, (state_order, state_order), jnp.float32, -spread, spread)
    symmetric = 0.5 * (uniform_part + uniform_part.T)
    diagonal = jax.random.uniform(diag_key, (state_order,), jnp.float32, 2.0, 3.0)
    positions = jnp.arange(state_order)
    matrix = symmetric.at[positions, positions].set(diagonal)
    return matrix


def draw_obs_cell(key, part):
    first_key, second_key, third_key, fourth_key = jax.random.split(jax.random.fold_in(key, 13), 4)

    def one_column(order_key, fill_key):
        ranks = jax.random.permutation(order_key, MEASURE_TOTAL)
        filler = jax.random.randint(fill_key, (MEASURE_TOTAL,), 0, GRID - 1)
        return jnp.where(ranks < GRID - 1, ranks, filler)
    return jnp.stack([one_column(first_key, second_key), one_column(third_key, fourth_key)], axis=1).astype(jnp.int32)


def setup_inputs(seed: int = 0) -> dict:
    seeds = jax.random.split(jax.random.key(seed), 6)
    return {
        "prior_covariance": draw_prior_covariance(jax.random.fold_in(seeds[5], 71), 0),
        "vel_first": jnp.clip(jax.random.uniform(seeds[1], (GRID, GRID), jnp.float32, -0.25, 0.25), -0.25, 0.25),
        "vel_second": jnp.clip(jax.random.uniform(seeds[2], (GRID, GRID), jnp.float32, -0.25, 0.25), -0.25, 0.25),
        "obs_cell": draw_obs_cell(jax.random.fold_in(seeds[5], 71), 0),
        "obs_noise": jnp.clip(jnp.exp(jax.random.uniform(seeds[4], (MEASURE_TOTAL,), jnp.float32, math.log(0.1), math.log(1.0))), 0.1, 1.0),
    }


dispersion = 0.125
centre_weight = 1.0 - 4.0 * dispersion
interp_weights = (0.42, 0.28, 0.18, 0.12)
finest_accuracy = lax.Precision.HIGHEST

def stencil_weights(vel_first, vel_second):
    return (dispersion - 0.5 * vel_first, dispersion + 0.5 * vel_first, dispersion - 0.5 * vel_second, dispersion + 0.5 * vel_second)

def sweep(field, weights):
    toward_next, toward_prev, across_next, across_prev = weights
    zero_first = jnp.zeros_like(field[:, :1])
    next_first = jnp.concatenate([field[:, 1:], zero_first], axis=1)
    prev_first = jnp.concatenate([zero_first, field[:, :-1]], axis=1)
    zero_second = jnp.zeros_like(field[:, :, :1])
    next_second = jnp.concatenate([field[:, :, 1:], zero_second], axis=2)
    prev_second = jnp.concatenate([zero_second, field[:, :, :-1]], axis=2)
    return centre_weight * field + toward_next * next_first + toward_prev * prev_first + across_next * next_second + across_prev * prev_second

def reference(prior_covariance, vel_first, vel_second, obs_cell, obs_noise):
    weights = tuple((weight_field[None, :, :, None] for weight_field in stencil_weights(vel_first, vel_second)))
    slab_count = 16
    slab_width = SYSTEM_ORDER // slab_count
    left_parts = []
    for slab_index in range(slab_count):
        column_slab = prior_covariance[:, slab_index * slab_width:(slab_index + 1) * slab_width]
        moved = sweep(column_slab.reshape(1, GRID, GRID, slab_width), weights)
        left_parts.append(moved.reshape(SYSTEM_ORDER, slab_width))
    propagated_covariance = jnp.concatenate(left_parts, axis=1)
    trailing_blocks = []
    for slab_index in range(slab_count):
        row_slab = propagated_covariance[slab_index * slab_width:(slab_index + 1) * slab_width]
        moved = sweep(row_slab.reshape(slab_width, GRID, GRID, 1), weights)
        trailing_blocks.append(moved.reshape(slab_width, SYSTEM_ORDER))
    prior_mean_vector = jnp.concatenate(trailing_blocks, axis=0)
    corner = obs_cell[:, 0] * GRID + obs_cell[:, 1]
    measured_sites = jnp.stack([corner, corner + 1, corner + GRID, corner + GRID + 1]).astype(jnp.int32)
    interp = jnp.array(interp_weights, jnp.float32)[:, None]
    chosen_entries = jnp.take(prior_mean_vector, measured_sites.reshape(-1), axis=1).reshape(SYSTEM_ORDER, 4, MEASURE_TOTAL)
    gain_panel = jnp.sum(chosen_entries * interp[None], axis=1)
    rows_pick = jnp.take(gain_panel, measured_sites.reshape(-1), axis=0).reshape(4, MEASURE_TOTAL, MEASURE_TOTAL)
    innovation = jnp.sum(rows_pick * interp[:, :, None], axis=0) + jnp.diag(obs_noise)
    symmetric = 0.5 * (innovation + innovation.T)
    factor = jnp.linalg.cholesky(symmetric)
    inverse = jax.scipy.linalg.solve_triangular(factor, jnp.eye(MEASURE_TOTAL, dtype=jnp.float32), lower=True)
    block_refresh = jnp.dot(gain_panel.astype(jnp.float32), inverse.T.astype(jnp.float32), precision=finest_accuracy, preferred_element_type=jnp.float32)
    return prior_mean_vector - jnp.dot(block_refresh.astype(jnp.float32), block_refresh.T.astype(jnp.float32), precision=finest_accuracy, preferred_element_type=jnp.float32)
```

```python
import functools
import jax
import jax.numpy as jnp
from jax import lax
from jax.experimental import pallas as pl
from jax.experimental.pallas import tpu as pltpu
from jax.sharding import PartitionSpec as P

HI = lax.Precision.HIGHEST
F32, BF16 = jnp.float32, jnp.bfloat16
dispersion = 0.125
centre_weight = 1.0 - 4.0 * dispersion
interp_weights = (0.42, 0.28, 0.18, 0.12)

def split(x):
    hi = x.astype(BF16)
    return hi, (x - hi.astype(F32)).astype(BF16)

def dot3(a, b, dims):
    (ah, al), (bh, bl) = a, b
    dg = functools.partial(lax.dot_general, dimension_numbers=(dims, ((), ())), preferred_element_type=F32)
    return dg(ah, bh) + (dg(ah, bl) + dg(al, bh))

def observed_weights(velf_ref, vels_ref, oi, oj):
    cells, count = velf_ref.shape[0], oi.shape[1]
    cid = lax.broadcasted_iota(jnp.int32, (cells, count), 0)
    w = {}
    def add(di, dj, v):
        w[di, dj] = w[di, dj] + v if (di, dj) in w else v
    for a in (0, 1):
        pick = jnp.where(cid == oi + a, 1.0, 0.0).astype(F32)
        by_j = [lax.dot_general(v[...], pick, (((0,), (0,)), ((), ())), precision=HI, preferred_element_type=F32)
                for v in (velf_ref, vels_ref)]
        for b in (0, 1):
            here = cid == oj + b
            vf, vs = [jnp.sum(jnp.where(here, x, 0.0), axis=0, keepdims=True) for x in by_j]
            h = interp_weights[2 * a + b]
            add(a, b, jnp.full_like(vf, h * centre_weight))
            add(a + 1, b, h * (dispersion - 0.5 * vf))
            add(a - 1, b, h * (dispersion + 0.5 * vf))
            add(a, b + 1, h * (dispersion - 0.5 * vs))
            add(a, b - 1, h * (dispersion + 0.5 * vs))
    return w

def line_weights(w, oi, oj, line, cells):
    count = oi.shape[1]
    jid = lax.broadcasted_iota(jnp.int32, (cells, count), 0)
    out = jnp.zeros((cells, count), F32)
    for dj in (-1, 0, 1, 2):
        row = jnp.zeros((1, count), F32)
        for di in (-1, 0, 1, 2):
            if (di, dj) in w:
                row = row + jnp.where(oi + di == line, w[di, dj], 0.0)
        out = jnp.where(jid == oj + dj, row, out)
    return out

def t_kernel(place_ref, p_hbm, velf_ref, vels_ref, oi_ref, oj_ref, t_ref, s_ref, buf, ch, cl, wsc, sems, *, tile):
    rows, cols = p_hbm.shape
    cells = velf_ref.shape[0]
    steps = rows // tile
    def fetch(n):
        return pltpu.make_async_copy(p_hbm.at[pl.ds(n * tile, tile), :], buf.at[n], sems.at[n])
    for n in range(steps):
        fetch(n).start()
    oi, oj = oi_ref[...], oj_ref[...]
    w = observed_weights(velf_ref, vels_ref, oi, oj)
    first_row, first_col = place_ref[0], place_ref[1]
    keys = sorted(w)
    for n, key in enumerate(keys):
        wsc[n:n + 1, :] = w[key]
    def build(l, _):
        ww = {key: wsc[n:n + 1, :] for n, key in enumerate(keys)}
        hi, lo = split(line_weights(ww, oi_ref[...], oj_ref[...], first_col + l, cells))
        at = pl.multiple_of(l * cells, cells)
        ch[pl.ds(at, cells), :] = hi
        cl[pl.ds(at, cells), :] = lo
        return 0
    lax.fori_loop(0, cols // cells, build, 0)
    s_ref[...] = jnp.zeros_like(s_ref)
    lines = tile // cells
    def run(n, _):
        pltpu.make_async_copy(p_hbm.at[pl.ds(n * tile, tile), :], buf.at[n], sems.at[n]).wait()
        t = dot3(split(buf[n]), (ch[...], cl[...]), ((1,), (0,)))
        t_ref[pl.ds(pl.multiple_of(n * tile, tile), tile), :] = t
        ww = {key: wsc[m:m + 1, :] for m, key in enumerate(keys)}
        c = jnp.concatenate([line_weights(ww, oi_ref[...], oj_ref[...], first_row + n * lines + m, cells)
                             for m in range(lines)], axis=0)
        s_ref[...] += dot3(split(c), split(t), ((0,), (0,)))
        return 0
    lax.fori_loop(0, steps, run, 0)

def partials(place, p, velf, vels, oi, oj, tile=256):
    rows, cols = p.shape
    count = oi.shape[1]
    v = pl.BlockSpec(memory_space=pltpu.VMEM)
    return pl.pallas_call(functools.partial(t_kernel, tile=tile),
        out_shape=(jax.ShapeDtypeStruct((rows, count), F32), jax.ShapeDtypeStruct((count, count), F32)),
        in_specs=[pl.BlockSpec(memory_space=pltpu.SMEM), pl.BlockSpec(memory_space=pl.ANY), v, v, v, v],
        out_specs=(v, v),
        scratch_shapes=[pltpu.VMEM((rows // tile, tile, cols), F32), pltpu.VMEM((cols, count), BF16),
                        pltpu.VMEM((cols, count), BF16), pltpu.VMEM((16, count), F32),
                        pltpu.SemaphoreType.DMA((rows // tile,))],
        compiler_params=pltpu.CompilerParams(vmem_limit_bytes=60 << 20),
        cost_estimate=pl.CostEstimate(flops=8 * 10**9, bytes_accessed=12 << 20, transcendentals=0),
    )(place, p, velf, vels, oi, oj)


def left_sweep(prev, mid, nxt, w):
    cells = mid.shape[0]
    up = pltpu.roll(mid, cells - 1, 0)
    down = pltpu.roll(mid, 1, 0)
    return centre_weight * mid + w[0] * nxt + w[1] * prev + w[2] * up + w[3] * down

def f_kernel(wl_ref, wr_ref, top_ref, p_prev, p_mid, p_next, bot_ref, lo_ref, hi_ref, f_ref, q_ref):
    n = pl.program_id(0)
    last = pl.num_programs(0) - 1
    cells = p_mid.shape[0]
    cols = p_mid.shape[1]
    lines = cols // cells
    at = pl.multiple_of(n * cells, cells)
    wide = [jnp.broadcast_to(wl_ref[:, m:m + 1], (cells, cells)) for m in range(4)]
    def side(ref):
        return [ref[pl.ds(at + d * cells, cells), :] for d in (0, 1, 2)]
    q_ref[:, 0:cells] = left_sweep(*side(lo_ref), wide)
    q_ref[:, (lines + 1) * cells:] = left_sweep(*side(hi_ref), wide)
    for l in range(lines):
        s = slice(l * cells, (l + 1) * cells)
        prev = jnp.where(n == 0, top_ref[:, s], p_prev[:, s])
        nxt = jnp.where(n == last, bot_ref[:, s], p_next[:, s])
        q_ref[:, (l + 1) * cells:(l + 2) * cells] = left_sweep(prev, p_mid[:, s], nxt, wide)
    for l in range(lines):
        mid = q_ref[:, (l + 1) * cells:(l + 2) * cells]
        s = slice(l * cells, (l + 1) * cells)
        f_ref[:, s] = (centre_weight * mid + wr_ref[0:1, s] * q_ref[:, (l + 2) * cells:(l + 3) * cells]
                       + wr_ref[1:2, s] * q_ref[:, l * cells:(l + 1) * cells]
                       + wr_ref[2:3, s] * pltpu.roll(mid, cells - 1, 1) + wr_ref[3:4, s] * pltpu.roll(mid, 1, 1))

def forecast(wl, wr, top, p, bot, lo, hi, cells):
    rows, cols = p.shape
    steps = rows // cells
    whole = lambda x: pl.BlockSpec(x.shape, lambda n: (0, 0), pipeline_mode=pl.Buffered(1))
    blk = lambda f: pl.BlockSpec((cells, cols), f)
    return pl.pallas_call(f_kernel, grid=(steps,),
        out_shape=jax.ShapeDtypeStruct((rows, cols), F32),
        in_specs=[pl.BlockSpec((cells, 4), lambda n: (n, 0)), whole(wr), whole(top),
                  blk(lambda n: (jnp.maximum(n - 1, 0), 0)), blk(lambda n: (n, 0)),
                  blk(lambda n: (jnp.minimum(n + 1, steps - 1), 0)), whole(bot), whole(lo), whole(hi)],
        out_specs=blk(lambda n: (n, 0)),
        scratch_shapes=[pltpu.VMEM((cells, cols + 2 * cells), F32)],
        compiler_params=pltpu.CompilerParams(vmem_limit_bytes=40 << 20),
        cost_estimate=pl.CostEstimate(flops=5 * 10**7, bytes_accessed=32 << 20, transcendentals=0),
    )(wl, wr, top, p, p, p, bot, lo, hi)

def fin_kernel(f_ref, g_ref, s_ref, gc_ref, o_ref, wh, wlo):
    @pl.when(pl.program_id(0) == 0)
    def _():
        w = jnp.dot(g_ref[...], s_ref[...], precision=HI, preferred_element_type=F32)
        h, l = split(w)
        wh[...] = h
        wlo[...] = l
    o_ref[...] = f_ref[...] - dot3((wh[...], wlo[...]), split(gc_ref[...]), ((1,), (1,)))

def finish(f, g, s, gc, tile=256):
    rows, cols = f.shape
    count = s.shape[0]
    whole = lambda x: pl.BlockSpec(x.shape, lambda n: (0, 0), pipeline_mode=pl.Buffered(1))
    return pl.pallas_call(fin_kernel, grid=(cols // tile,),
        out_shape=jax.ShapeDtypeStruct((rows, cols), F32),
        in_specs=[pl.BlockSpec((rows, tile), lambda n: (0, n)), whole(g), whole(s), pl.BlockSpec((tile, count), lambda n: (n, 0))],
        out_specs=pl.BlockSpec((rows, tile), lambda n: (0, n)),
        scratch_shapes=[pltpu.VMEM((rows, count), BF16), pltpu.VMEM((rows, count), BF16)],
        compiler_params=pltpu.CompilerParams(vmem_limit_bytes=40 << 20),
        cost_estimate=pl.CostEstimate(flops=8 * 10**9, bytes_accessed=24 << 20, transcendentals=0),
    )(f, g, s, gc)


def pick_row(a, k):
    return jnp.broadcast_to(a[k:k + 1, :], a.shape)

def pick_col(a, k):
    return jnp.broadcast_to(a[:, k:k + 1], a.shape)

def invert_tile(a, pivots):
    n = a.shape[0]
    rid = lax.broadcasted_iota(jnp.int32, a.shape, 0)
    cid = lax.broadcasted_iota(jnp.int32, a.shape, 1)
    for k in range(0, n, pivots):
        if pivots == 1:
            row = a[k:k+1, :]
            col = pick_col(a, k)
            p = col[k:k+1, :]
            q = 1.0 / p
            r = row * q
            lane = cid[:1] == k
            r2 = jnp.where(lane, q, r)
            base = jnp.where(cid == k, 0.0, a)
            upd = base - col * r2
            a = jnp.where(rid == k, r2, upd)
        else:
            row0, row1 = a[k:k+1, :], a[k+1:k+2, :]
            col0, col1 = pick_col(a, k), pick_col(a, k + 1)
            p00, p10, p11 = col0[k:k+1, :], col0[k+1:k+2, :], col1[k+1:k+2, :]
            det = 1.0 / (p00 * p11 - p10 * p10)
            i00, i01, i11 = p11 * det, -p10 * det, p00 * det
            lane0, lane1 = cid[:1] == k, cid[:1] == k + 1
            r0 = jnp.where(lane0, i00, jnp.where(lane1, i01, i00 * row0 + i01 * row1))
            r1 = jnp.where(lane0, i01, jnp.where(lane1, i11, i01 * row0 + i11 * row1))
            base = jnp.where((cid == k) | (cid == k + 1), 0.0, a)
            upd = base - col0 * r0 - col1 * r1
            a = jnp.where(rid == k, r0, jnp.where(rid == k + 1, r1, upd))
    return a

def inv_kernel(s_ref, o_ref, *, pivots, block, prec=HI):
    n = s_ref.shape[0]
    s = s_ref[...]
    o_ref[...] = 0.5 * (s + s.T)
    nb = n // block

    def step(k, _):
        lo = pl.multiple_of(k * block, block)
        d = invert_tile(o_ref[pl.ds(lo, block), pl.ds(lo, block)], pivots)
        panel = o_ref[pl.ds(lo, block), :]
        col = o_ref[:, pl.ds(lo, block)]
        cid = lax.broadcasted_iota(jnp.int32, panel.shape, 1)
        dfull = jnp.concatenate([d] * nb, axis=1)
        inside = (cid >= lo) & (cid < lo + block)
        r = jnp.where(inside, dfull, jnp.dot(d, panel, precision=prec, preferred_element_type=jnp.float32))
        cid2 = lax.broadcasted_iota(jnp.int32, (n, n), 1)
        rest = jnp.where((cid2 >= lo) & (cid2 < lo + block), 0.0, o_ref[...])
        o_ref[...] = rest - jnp.dot(col, r, precision=prec, preferred_element_type=jnp.float32)
        o_ref[pl.ds(lo, block), :] = r
        return 0
    lax.fori_loop(0, nb, step, 0)

def invert(s, pivots=1, block=128):
    return pl.pallas_call(functools.partial(inv_kernel, pivots=pivots, block=block),
        out_shape=jax.ShapeDtypeStruct(s.shape, jnp.float32),
        in_specs=[pl.BlockSpec(memory_space=pltpu.VMEM)], out_specs=pl.BlockSpec(memory_space=pltpu.VMEM))(s)

def m_kernel(wl_ref, top_ref, t_ref, bot_ref, o_ref):
    cells, count = top_ref.shape
    lines = t_ref.shape[0] // cells
    for l in range(lines):
        s = slice(l * cells, (l + 1) * cells)
        wide = [jnp.broadcast_to(wl_ref[s, m:m + 1], (cells, count)) for m in range(4)]
        prev = top_ref[...] if l == 0 else t_ref[(l - 1) * cells:l * cells, :]
        nxt = bot_ref[...] if l == lines - 1 else t_ref[(l + 1) * cells:(l + 2) * cells, :]
        o_ref[s, :] = left_sweep(prev, t_ref[s, :], nxt, wide)


def sweep_panel(wl, top, t, bot):
    v = pl.BlockSpec(memory_space=pltpu.VMEM)
    return pl.pallas_call(m_kernel, out_shape=jax.ShapeDtypeStruct(t.shape, F32), in_specs=[v] * 4, out_specs=v,
        cost_estimate=pl.CostEstimate(flops=10**7, bytes_accessed=5 << 20, transcendentals=0))(wl, top, t, bot)


def sides(block, axis, dim, width):
    count = lax.axis_size(axis)
    forward = [(i, i + 1) for i in range(count - 1)]
    backward = [(target, source) for source, target in forward]
    low = lax.ppermute(lax.slice_in_dim(block, block.shape[dim] - width, None, axis=dim), axis, forward)
    high = lax.ppermute(lax.slice_in_dim(block, 0, width, axis=dim), axis, backward)
    return low, high


def cell_weights(vel_first, vel_second, start, lines):
    first = lax.dynamic_slice_in_dim(vel_first, start, lines, 0)
    second = lax.dynamic_slice_in_dim(vel_second, start, lines, 0)
    at = lax.broadcasted_iota(jnp.int32, second.shape, 1)
    ends = second.shape[1] - 1
    return [w.reshape(-1) for w in (
        dispersion - 0.5 * first,
        dispersion + 0.5 * first,
        jnp.where(at == ends, 0.0, dispersion - 0.5 * second),
        jnp.where(at == 0, 0.0, dispersion + 0.5 * second))]


def body(prior, vel_first, vel_second, obs_cell, obs_noise):
    rows, cols = prior.shape
    cells = vel_first.shape[0]
    row_lines, col_lines = rows // cells, cols // cells
    row_place, col_place = lax.axis_index("row"), lax.axis_index("col")
    row_count, col_count = lax.axis_size("row"), lax.axis_size("col")
    place = jnp.stack([row_place * row_lines, col_place * col_lines]).astype(jnp.int32)
    wl = jnp.stack(cell_weights(vel_first, vel_second, row_place * row_lines, row_lines), axis=1)
    wr = jnp.stack(cell_weights(vel_first, vel_second, col_place * col_lines, col_lines), axis=0)
    oi, oj = obs_cell[:, 0][None], obs_cell[:, 1][None]

    t_part, s_part = partials(place, prior, vel_first, vel_second, oi, oj)
    s_total = lax.psum(s_part, ("row", "col"))
    t_top, t_bot = sides(t_part, "row", 0, cells)
    g_part = sweep_panel(wl, t_top, t_part, t_bot)
    g_line = lax.psum_scatter(g_part, "col", scatter_dimension=0, tiled=True)
    blocks = cols // rows
    perm = []
    for r in range(row_count):
        for c in range(col_count):
            perm.append((r * col_count + c, ((r % blocks) * col_count + c) * col_count + r // blocks))
    g_rows = lax.all_gather(g_line, "col", axis=0, tiled=True)
    g_cols = lax.all_gather(lax.ppermute(g_line, ("row", "col"), perm), "row", axis=0, tiled=True)

    lo, hi = sides(prior, "col", 1, cells)
    top, bot = sides(prior, "row", 0, cells)
    lo_top, lo_bot = sides(lo, "row", 0, cells)
    hi_top, hi_bot = sides(hi, "row", 0, cells)
    lo = jnp.concatenate([lo_top, lo, lo_bot], axis=0)
    hi = jnp.concatenate([hi_top, hi, hi_bot], axis=0)
    field = forecast(wl, wr, top, prior, bot, lo, hi, cells)

    s_inv = invert(s_total + jnp.diag(obs_noise), 2, 128)
    return finish(field, g_rows, s_inv, g_cols, tile=512)


def solution(mesh):
    placed = (P("row", "col"), P(), P(), P(), P())
    return jax.shard_map(body, mesh=mesh, in_specs=placed, out_specs=P("row", "col"), check_vma=False)
```

```python
import functools
import jax
import jax.numpy as jnp
from jax import lax
from jax.experimental import pallas as pl
from jax.experimental.pallas import tpu as pltpu
from jax.sharding import PartitionSpec as P

HI = lax.Precision.HIGHEST
F32, BF16 = jnp.float32, jnp.bfloat16
dispersion = 0.125
centre_weight = 1.0 - 4.0 * dispersion
interp_weights = (0.42, 0.28, 0.18, 0.12)

def split(x):
    hi = x.astype(BF16)
    return hi, (x - hi.astype(F32)).astype(BF16)

def dot3(a, b, dims):
    (ah, al), (bh, bl) = a, b
    dg = functools.partial(lax.dot_general, dimension_numbers=(dims, ((), ())), preferred_element_type=F32)
    return dg(ah, bh) + (dg(ah, bl) + dg(al, bh))

def observed_weights(velf_ref, vels_ref, oi, oj):
    cells, count = velf_ref.shape[0], oi.shape[1]
    cid = lax.broadcasted_iota(jnp.int32, (cells, count), 0)
    w = {}
    def add(di, dj, v):
        w[di, dj] = w[di, dj] + v if (di, dj) in w else v
    for a in (0, 1):
        pick = jnp.where(cid == oi + a, 1.0, 0.0).astype(F32)
        by_j = [lax.dot_general(v[...], pick, (((0,), (0,)), ((), ())), precision=HI, preferred_element_type=F32)
                for v in (velf_ref, vels_ref)]
        for b in (0, 1):
            here = cid == oj + b
            vf, vs = [jnp.sum(jnp.where(here, x, 0.0), axis=0, keepdims=True) for x in by_j]
            h = interp_weights[2 * a + b]
            add(a, b, jnp.full_like(vf, h * centre_weight))
            add(a + 1, b, h * (dispersion - 0.5 * vf))
            add(a - 1, b, h * (dispersion + 0.5 * vf))
            add(a, b + 1, h * (dispersion - 0.5 * vs))
            add(a, b - 1, h * (dispersion + 0.5 * vs))
    return w

def line_weights(w, oi, oj, line, cells):
    count = oi.shape[1]
    jid = lax.broadcasted_iota(jnp.int32, (cells, count), 0)
    out = jnp.zeros((cells, count), F32)
    for dj in (-1, 0, 1, 2):
        row = jnp.zeros((1, count), F32)
        for di in (-1, 0, 1, 2):
            if (di, dj) in w:
                row = row + jnp.where(oi + di == line, w[di, dj], 0.0)
        out = jnp.where(jid == oj + dj, row, out)
    return out

def observed_panel(first_row, first_col, p_hbm, velf_ref, vels_ref, oi_ref, oj_ref, t_ref, s_ref, buf, ch, cl, wsc, sems):
    rows, cols = p_hbm.shape
    tile = buf.shape[1]
    cells = velf_ref.shape[0]
    steps = rows // tile
    def fetch(n):
        return pltpu.make_async_copy(p_hbm.at[pl.ds(n * tile, tile), :], buf.at[n], sems.at[n])
    for n in range(steps):
        fetch(n).start()
    oi, oj = oi_ref[...], oj_ref[...]
    w = observed_weights(velf_ref, vels_ref, oi, oj)
    keys = sorted(w)
    for n, key in enumerate(keys):
        wsc[n:n + 1, :] = w[key]
    def build(l, _):
        ww = {key: wsc[n:n + 1, :] for n, key in enumerate(keys)}
        hi, lo = split(line_weights(ww, oi_ref[...], oj_ref[...], first_col + l, cells))
        at = pl.multiple_of(l * cells, cells)
        ch[pl.ds(at, cells), :] = hi
        cl[pl.ds(at, cells), :] = lo
        return 0
    lax.fori_loop(0, cols // cells, build, 0)
    s_ref[...] = jnp.zeros_like(s_ref)
    lines = tile // cells
    def run(n, _):
        pltpu.make_async_copy(p_hbm.at[pl.ds(n * tile, tile), :], buf.at[n], sems.at[n]).wait()
        t = dot3(split(buf[n]), (ch[...], cl[...]), ((1,), (0,)))
        t_ref[pl.ds(pl.multiple_of(n * tile, tile), tile), :] = t
        ww = {key: wsc[m:m + 1, :] for m, key in enumerate(keys)}
        c = jnp.concatenate([line_weights(ww, oi_ref[...], oj_ref[...], first_row + n * lines + m, cells)
                             for m in range(lines)], axis=0)
        s_ref[...] += dot3(split(c), split(t), ((0,), (0,)))
        return 0
    lax.fori_loop(0, steps, run, 0)


def left_sweep(prev, mid, nxt, w):
    cells = mid.shape[0]
    up = pltpu.roll(mid, cells - 1, 0)
    down = pltpu.roll(mid, 1, 0)
    return centre_weight * mid + w[0] * nxt + w[1] * prev + w[2] * up + w[3] * down

def f_kernel(wl_ref, wr_ref, top_ref, p_prev, p_mid, p_next, bot_ref, lo_ref, hi_ref, f_ref, q_ref):
    n = pl.program_id(0)
    last = pl.num_programs(0) - 1
    cells = p_mid.shape[0]
    cols = p_mid.shape[1]
    lines = cols // cells
    at = pl.multiple_of(n * cells, cells)
    wide = [jnp.broadcast_to(wl_ref[:, m:m + 1], (cells, cells)) for m in range(4)]
    def side(ref):
        return [ref[pl.ds(at + d * cells, cells), :] for d in (0, 1, 2)]
    q_ref[:, 0:cells] = left_sweep(*side(lo_ref), wide)
    q_ref[:, (lines + 1) * cells:] = left_sweep(*side(hi_ref), wide)
    for l in range(lines):
        s = slice(l * cells, (l + 1) * cells)
        prev = jnp.where(n == 0, top_ref[:, s], p_prev[:, s])
        nxt = jnp.where(n == last, bot_ref[:, s], p_next[:, s])
        q_ref[:, (l + 1) * cells:(l + 2) * cells] = left_sweep(prev, p_mid[:, s], nxt, wide)
    for l in range(lines):
        mid = q_ref[:, (l + 1) * cells:(l + 2) * cells]
        s = slice(l * cells, (l + 1) * cells)
        f_ref[:, s] = (centre_weight * mid + wr_ref[0:1, s] * q_ref[:, (l + 2) * cells:(l + 3) * cells]
                       + wr_ref[1:2, s] * q_ref[:, l * cells:(l + 1) * cells]
                       + wr_ref[2:3, s] * pltpu.roll(mid, cells - 1, 1) + wr_ref[3:4, s] * pltpu.roll(mid, 1, 1))

def forecast(wl, wr, top, p, bot, lo, hi, cells):
    rows, cols = p.shape
    steps = rows // cells
    whole = lambda x: pl.BlockSpec(x.shape, lambda n: (0, 0), pipeline_mode=pl.Buffered(1))
    blk = lambda f: pl.BlockSpec((cells, cols), f)
    return pl.pallas_call(f_kernel, grid=(steps,),
        out_shape=jax.ShapeDtypeStruct((rows, cols), F32),
        in_specs=[pl.BlockSpec((cells, 4), lambda n: (n, 0)), whole(wr), whole(top),
                  blk(lambda n: (jnp.maximum(n - 1, 0), 0)), blk(lambda n: (n, 0)),
                  blk(lambda n: (jnp.minimum(n + 1, steps - 1), 0)), whole(bot), whole(lo), whole(hi)],
        out_specs=blk(lambda n: (n, 0)),
        scratch_shapes=[pltpu.VMEM((cells, cols + 2 * cells), F32)],
        compiler_params=pltpu.CompilerParams(vmem_limit_bytes=40 << 20),
        cost_estimate=pl.CostEstimate(flops=5 * 10**7, bytes_accessed=32 << 20, transcendentals=0),
    )(wl, wr, top, p, p, p, bot, lo, hi)

def fin_kernel(f_ref, g_ref, s_ref, gc_ref, o_ref, wh, wlo):
    @pl.when(pl.program_id(0) == 0)
    def _():
        w = jnp.dot(g_ref[...], s_ref[...], precision=HI, preferred_element_type=F32)
        h, l = split(w)
        wh[...] = h
        wlo[...] = l
    o_ref[...] = f_ref[...] - dot3((wh[...], wlo[...]), split(gc_ref[...]), ((1,), (1,)))

def finish(f, g, s, gc, tile=256):
    rows, cols = f.shape
    count = s.shape[0]
    whole = lambda x: pl.BlockSpec(x.shape, lambda n: (0, 0), pipeline_mode=pl.Buffered(1))
    return pl.pallas_call(fin_kernel, grid=(cols // tile,),
        out_shape=jax.ShapeDtypeStruct((rows, cols), F32),
        in_specs=[pl.BlockSpec((rows, tile), lambda n: (0, n)), whole(g), whole(s), pl.BlockSpec((tile, count), lambda n: (n, 0))],
        out_specs=pl.BlockSpec((rows, tile), lambda n: (0, n)),
        scratch_shapes=[pltpu.VMEM((rows, count), BF16), pltpu.VMEM((rows, count), BF16)],
        compiler_params=pltpu.CompilerParams(vmem_limit_bytes=40 << 20),
        cost_estimate=pl.CostEstimate(flops=8 * 10**9, bytes_accessed=24 << 20, transcendentals=0),
    )(f, g, s, gc)


def invert_in(s_ref, noise_ref, o_ref, hooks, block=128):
    n = s_ref.shape[0]
    s = s_ref[...]
    rid = lax.broadcasted_iota(jnp.int32, (n, n), 0)
    cid = lax.broadcasted_iota(jnp.int32, (n, n), 1)
    o_ref[...] = 0.5 * (s + s.T) + jnp.where(rid == cid, noise_ref[...], 0.0)
    nb = n // block
    for k in range(nb):
        lo = k * block
        own = slice(lo, lo + block)
        a = o_ref[own, own]
        for part in (0, 1):
            if (k, part) in hooks:
                hooks[k, part]()
            a = pivot(a, range(part * block // 2, (part + 1) * block // 2, 2))
        panel = jnp.dot(a, o_ref[own, :], precision=HI, preferred_element_type=F32)
        col = o_ref[:, own]
        for j in range(nb):
            here = slice(j * block, (j + 1) * block)
            r = a if j == k else panel[:, here]
            upd = jnp.dot(col, r, precision=HI, preferred_element_type=F32)
            o_ref[:, here] = -upd if j == k else o_ref[:, here] - upd
            o_ref[own, here] = r


def pivot(a, steps):
    rid = lax.broadcasted_iota(jnp.int32, a.shape, 0)
    cid = lax.broadcasted_iota(jnp.int32, a.shape, 1)
    for k in steps:
        row0, row1 = a[k:k + 1, :], a[k + 1:k + 2, :]
        col0 = jnp.broadcast_to(a[:, k:k + 1], a.shape)
        col1 = jnp.broadcast_to(a[:, k + 1:k + 2], a.shape)
        p00, p10, p11 = col0[k:k + 1, :], col0[k + 1:k + 2, :], col1[k + 1:k + 2, :]
        det = 1.0 / (p00 * p11 - p10 * p10)
        i00, i01, i11 = p11 * det, -p10 * det, p00 * det
        lane0, lane1 = cid[:1] == k, cid[:1] == k + 1
        r0 = jnp.where(lane0, i00, jnp.where(lane1, i01, i00 * row0 + i01 * row1))
        r1 = jnp.where(lane0, i01, jnp.where(lane1, i11, i01 * row0 + i11 * row1))
        base = jnp.where((cid == k) | (cid == k + 1), 0.0, a)
        upd = base - col0 * r0 - col1 * r1
        a = jnp.where(rid == k, r0, jnp.where(rid == k + 1, r1, upd))
    return a


MESH = pl.DeviceIdType.MESH
RING = 4


def exchange_kernel(p_hbm, velf_ref, vels_ref, oi_ref, oj_ref, noise_ref, wl_ref,
                    sinv_ref, grow_ref, gcol_ref, top_ref, bot_ref, lo_ref, hi_ref,
                    buf, ch, cl, wsc, t_ref, s_ref, th, gp, rg, gs, ry, rl,
                    s_acc, r0, r1, r2, r3, s_out, in_sems, send_sems, recv_sems):
    rows, cols = p_hbm.shape
    cells, count = th.shape[1], th.shape[2]
    row, col = lax.axis_index("row"), lax.axis_index("col")
    row_count, col_count = lax.axis_size("row"), lax.axis_size("col")
    x, z = row // RING, row % RING
    y, core = col // 2, col % 2

    def step(v, d):
        return (v + d + RING) % RING

    def chip(dx=0, dy=0, dz=0):
        return (step(x, dx) * RING + step(z, dz), step(y, dy) * 2 + core)

    partner = (row, col + 1 - 2 * core)
    twin_row = y * RING + 2 * core + z % 2
    twin_col = 2 * x + z // 2
    twin = (twin_row, twin_col)
    alone = (twin_row == row) & (twin_col == col)
    up, down = (row + 1) % row_count, (row + row_count - 1) % row_count
    right, left = (col + 1) % col_count, (col + col_count - 1) % col_count

    barrier = pltpu.get_barrier_semaphore()
    greeted = [partner, (up, col), (down, col), (row, right), (row, left),
               (up, right), (up, left), (down, right), (down, left)]
    greeted += [chip(dx=d) for d in (1, 2, 3)] + [chip(dy=d) for d in (1, 2, 3)] + [chip(dz=d) for d in (1, 2, 3)]
    for peer in greeted:
        pl.semaphore_signal(barrier, inc=1, device_id=peer, device_id_type=MESH)

    @pl.when(jnp.logical_not(alone))
    def _():
        pl.semaphore_signal(barrier, inc=1, device_id=twin, device_id_type=MESH)
    pl.semaphore_wait(barrier, len(greeted) + 1 - alone.astype(jnp.int32))

    used, sent = {}, []

    def slot(key):
        if key not in used:
            used[key] = len(used)
        return used[key]

    def copy(key, src, dst, peer):
        n = slot(key)
        return pltpu.make_async_remote_copy(src_ref=src, dst_ref=dst, send_sem=send_sems.at[n], recv_sem=recv_sems.at[n],
                                            device_id=peer, device_id_type=MESH)

    def send(key, src, dst, peer):
        c = copy(key, src, dst, peer)
        c.start()
        sent.append(c)

    def arrive(key, dst, peer):
        copy(key, dst, dst, peer).wait_recv()

    mid = pl.ds(cells, rows)
    halo = [
        ("p_up", p_hbm.at[pl.ds(rows - cells, cells), :], top_ref.at[:, :], (up, col), (down, col)),
        ("p_down", p_hbm.at[pl.ds(0, cells), :], bot_ref.at[:, :], (down, col), (up, col)),
        ("p_right", p_hbm.at[:, pl.ds(cols - cells, cells)], lo_ref.at[mid, :], (row, right), (row, left)),
        ("p_left", p_hbm.at[:, pl.ds(0, cells)], hi_ref.at[mid, :], (row, left), (row, right)),
        ("p_up_right", p_hbm.at[pl.ds(rows - cells, cells), pl.ds(cols - cells, cells)], lo_ref.at[pl.ds(0, cells), :],
         (up, right), (down, left)),
        ("p_up_left", p_hbm.at[pl.ds(rows - cells, cells), pl.ds(0, cells)], hi_ref.at[pl.ds(0, cells), :],
         (up, left), (down, right)),
        ("p_down_right", p_hbm.at[pl.ds(0, cells), pl.ds(cols - cells, cells)], lo_ref.at[pl.ds(rows + cells, cells), :],
         (down, right), (up, left)),
        ("p_down_left", p_hbm.at[pl.ds(0, cells), pl.ds(0, cells)], hi_ref.at[pl.ds(rows + cells, cells), :],
         (down, left), (up, right)),
    ]
    for key, src, dst, to, _ in halo:
        send(key, src, dst, to)

    observed_panel(row * (rows // cells), col * (cols // cells), p_hbm, velf_ref, vels_ref, oi_ref, oj_ref, t_ref, s_ref,
                   buf, ch, cl, wsc, in_sems)

    send("t_up", t_ref.at[pl.ds(rows - cells, cells), :], th.at[0], (up, col))
    send("t_down", t_ref.at[pl.ds(0, cells), :], th.at[1], (down, col))
    half = count // 2
    mine = pl.multiple_of(core * half, half)
    other = pl.multiple_of(half - core * half, half)
    send("s_core", s_ref.at[pl.ds(other, half), :], r0.at[:, :], partner)
    arrive("s_core", r0.at[:, :], partner)
    s_acc[pl.ds(mine, half), :] = s_ref[pl.ds(mine, half), :] + r0[...]

    wide = count // 2
    p1, p2, p3 = half // RING, half // RING**2, 8
    order = (("x", "z"), ("z", "x"))
    pos = {"x": x, "y": y, "z": z}

    def at1(a, i):
        return (pl.ds(pl.multiple_of(mine + i * p1, 8), p1), pl.ds(a * wide, wide))

    def at2(a, i, j):
        return (pl.ds(pl.multiple_of(mine + i * p1 + j * p2, 8), p2), pl.ds(a * wide, wide))

    def at3(a, i, j, q):
        return (pl.ds(pl.multiple_of(mine + i * p1 + j * p2 + (q // 2) * p3, 8), p3),
                pl.ds(pl.multiple_of(a * wide + (q % 2) * 128, 128), 128))

    def hop(axis, d):
        return chip(**{"d" + axis: d})

    def reduce_start(name, slots, place, axes):
        for a in (0, 1):
            for d in (1, 2, 3):
                axis = axes[a]
                send((name, a, d), s_acc.at[place(a, step(pos[axis], d))], slots.at[a, d - 1], hop(axis, d))

    def reduce_end(name, slots, place, axes):
        for a in (0, 1):
            for d in (1, 2, 3):
                arrive((name, a, d), slots.at[a, d - 1], hop(axes[a], -d))
            here = place(a, pos[axes[a]])
            s_acc[here] = (s_acc[here] + slots[a, 0]) + (slots[a, 1] + slots[a, 2])

    def gather_start(name, place, axes):
        for a in (0, 1):
            here = place(a, pos[axes[a]])
            for d in (1, 2, 3):
                send((name, a, d), s_out.at[here], s_out.at[here], hop(axes[a], d))

    def gather_end(name, place, axes):
        for a in (0, 1):
            for d in (1, 2, 3):
                there = place(a, step(pos[axes[a]], -d))
                arrive((name, a, d), s_out.at[there], hop(axes[a], -d))

    axes1, axes2, axes3 = [o[0] for o in order], [o[1] for o in order], ["y", "y"]
    own1 = [pos[a] for a in axes1]
    own2 = [pos[a] for a in axes2]
    place1 = at1
    place2 = lambda a, j: at2(a, own1[a], j)
    place3 = lambda a, q: at3(a, own1[a], own2[a], q)

    reduce_start("s1", r1, place1, axes1)

    arrive("t_up", th.at[0], (down, col))
    arrive("t_down", th.at[1], (up, col))
    lines = rows // cells
    for l in range(lines):
        s = slice(l * cells, (l + 1) * cells)
        w = [jnp.broadcast_to(wl_ref[s, m:m + 1], (cells, count)) for m in range(4)]
        prev = th[0] if l == 0 else t_ref[(l - 1) * cells:l * cells, :]
        nxt = th[1] if l == lines - 1 else t_ref[(l + 1) * cells:(l + 2) * cells, :]
        gp[l] = left_sweep(prev, t_ref[s, :], nxt, w)
    for q in range(RING):
        send(("g_core", q), gp.at[2 * q + 1 - core], rg.at[q], partner)

    reduce_end("s1", r1, place1, axes1)
    reduce_start("s2", r2, place2, axes2)

    for q in range(RING):
        arrive(("g_core", q), rg.at[q], partner)
        gs[q] = gp[2 * q + core] + rg[q]
    h = cells // 2
    first, second = pl.ds(0, h), pl.ds(h, h)
    far, nxt_y, prv_y = step(y, 2), step(y, 1), step(y, -1)
    send("g_far_up", gs.at[far, first], ry.at[0], chip(dy=1))
    send("g_far_down", gs.at[far, second], ry.at[1], chip(dy=-1))

    reduce_end("s2", r2, place2, axes2)
    reduce_start("s3", r3, place3, axes3)

    arrive("g_far_up", ry.at[0], chip(dy=-1))
    arrive("g_far_down", ry.at[1], chip(dy=1))
    gs[nxt_y, first] = gs[nxt_y, first] + ry[0]
    gs[prv_y, second] = gs[prv_y, second] + ry[1]
    send("g_up", gs.at[nxt_y], rl.at[0], chip(dy=1))
    send("g_down", gs.at[prv_y], rl.at[1], chip(dy=-1))

    for a in (0, 1):
        for d in (1, 2, 3):
            arrive(("s3", a, d), r3.at[a, d - 1], hop("y", -d))
        here = place3(a, y)
        s_out[here] = (s_acc[here] + r3[a, 0]) + (r3[a, 1] + r3[a, 2])
    gather_start("a3", place3, axes3)
    gather_end("a3", place3, axes3)
    gather_start("a2", place2, axes2)

    arrive("g_up", rl.at[0], chip(dy=-1))
    arrive("g_down", rl.at[1], chip(dy=1))

    def line_at(c, lo=0, n=cells):
        return (pl.ds(pl.multiple_of(c * cells + lo, 8), n), slice(None))

    own = line_at(col)
    grow_ref[own] = (gs[y] + rl[0]) + rl[1]

    def col_line(xx, zz, lo=0, n=cells):
        return line_at(8 * (zz % 2) + 2 * xx + zz // 2, lo, n)

    landing = col_line(x, z)
    away = line_at(8 * (row % 2) + col)
    twin_copy = copy("twin", grow_ref.at[own], gcol_ref.at[away], twin)

    @pl.when(alone)
    def _():
        gcol_ref[landing] = grow_ref[own]

    @pl.when(jnp.logical_not(alone))
    def _():
        twin_copy.start()

    send("y_up", grow_ref.at[own], grow_ref.at[own], chip(dy=1))
    send("y_down", grow_ref.at[own], grow_ref.at[own], chip(dy=-1))
    send(("c", 0), grow_ref.at[own], grow_ref.at[own], partner)

    gather_end("a2", place2, axes2)
    gather_start("a1", place1, axes1)
    gather_end("a1", place1, axes1)
    whole = (pl.ds(mine, half), slice(None))
    send("s_back", s_out.at[whole], s_out.at[whole], partner)

    def c_of(d):
        return 2 * step(y, d) + core

    def twin_landed():
        @pl.when(jnp.logical_not(alone))
        def _():
            arrive("twin", gcol_ref.at[landing], twin)

    lows = (0, h)
    rings = (("x", "z"), ("z", "x"))

    def piece(a, d0, d1, lo=0, n=h):
        dx, dz = (d0, d1) if a == 0 else (d1, d0)
        return gcol_ref.at[col_line(step(x, dx), step(z, dz), lows[a] + lo, n)]

    def turn(a, level, d):
        return hop(rings[a][level], d)

    def p1():
        twin_landed()
        for a in (0, 1):
            for d in (1, -1):
                send(("q1", a, d), piece(a, 0, 0), piece(a, 0, 0), turn(a, 0, d))
        for a in (0, 1):
            for d in (1, -1):
                send(("q2", a, 0, d), piece(a, 0, 0), piece(a, 0, 0), turn(a, 1, d))
        arrive("y_up", grow_ref.at[line_at(c_of(-1))], chip(dy=-1))
        arrive("y_down", grow_ref.at[line_at(c_of(1))], chip(dy=1))
        send("y_far_up", grow_ref.at[line_at(c_of(-1), 0, h)], grow_ref.at[line_at(c_of(-1), 0, h)], chip(dy=1))
        send("y_far_down", grow_ref.at[line_at(c_of(1), h, h)], grow_ref.at[line_at(c_of(1), h, h)], chip(dy=-1))
        for d in (-1, 1):
            send(("c", d), grow_ref.at[line_at(c_of(d))], grow_ref.at[line_at(c_of(d))], partner)

    def p2():
        for a in (0, 1):
            for d in (1, -1):
                arrive(("q1", a, d), piece(a, -d, 0), turn(a, 0, -d))
                lo = 0 if d == 1 else h // 2
                send(("q1r", a, d), piece(a, -d, 0, lo, h // 2), piece(a, -d, 0, lo, h // 2), turn(a, 0, d))
        for a in (0, 1):
            for k in (-1, 1):
                for d in (1, -1):
                    send(("q2", a, k, d), piece(a, k, 0), piece(a, k, 0), turn(a, 1, d))

    def p3():
        for a in (0, 1):
            for d in (1, -1):
                lo = 0 if d == 1 else h // 2
                arrive(("q1r", a, d), piece(a, -2 * d, 0, lo, h // 2), turn(a, 0, -d))
            for d in (1, -1):
                send(("q2", a, 2, d), piece(a, 2, 0), piece(a, 2, 0), turn(a, 1, d))

    def relay(a, k, d):
        arrive(("q2", a, k, d), piece(a, k, -d), turn(a, 1, -d))
        if (k in (0, -1)) == (d == 1):
            send(("q2r", a, k), piece(a, k, -d), piece(a, k, -d), turn(a, 1, d))

    def p4():
        for k in (0, -1, 1):
            for a in (0, 1):
                for d in (1, -1):
                    relay(a, k, d)
        arrive("y_far_up", grow_ref.at[line_at(c_of(-2), 0, h)], chip(dy=-1))
        arrive("y_far_down", grow_ref.at[line_at(c_of(2), h, h)], chip(dy=1))
        send(("c", 2), grow_ref.at[line_at(c_of(2))], grow_ref.at[line_at(c_of(2))], partner)

    def p5():
        for a in (0, 1):
            for d in (1, -1):
                relay(a, 2, d)

    hooks = {(0, 0): p1, (0, 1): p2, (1, 0): p3, (1, 1): p4, (2, 0): p5}

    arrive("s_back", s_out.at[pl.ds(other, half), :], partner)
    invert_in(s_out, noise_ref, sinv_ref, hooks)

    for key, _, dst, _, frm in halo:
        arrive(key, dst, frm)
    for d in (0, -1, 1, 2):
        there = line_at(2 * step(y, d) + 1 - core)
        arrive(("c", d), grow_ref.at[there], partner)
    for a in (0, 1):
        for k in (0, -1, 1, 2):
            d = 1 if k in (0, -1) else -1
            arrive(("q2r", a, k), piece(a, k, -2 * d), turn(a, 1, -d))
    for c in sent:
        c.wait_send()

    @pl.when(jnp.logical_not(alone))
    def _():
        twin_copy.wait_send()


def exchange(p, velf, vels, oi, oj, noise, wl, tile=256):
    rows, cols = p.shape
    count, cells = oi.shape[1], velf.shape[0]
    half = count // 2
    p1, p2 = half // RING, half // RING**2
    v = pl.BlockSpec(memory_space=pltpu.VMEM)
    hbm = pl.BlockSpec(memory_space=pl.ANY)
    shape = lambda *s: jax.ShapeDtypeStruct(s, F32)
    vmem = lambda *s: pltpu.VMEM(s, F32)
    return pl.pallas_call(exchange_kernel,
        out_shape=(shape(count, count), shape(rows, count), shape(cols, count), shape(cells, cols), shape(cells, cols),
                   shape(rows + 2 * cells, cells), shape(rows + 2 * cells, cells)),
        in_specs=[hbm, v, v, v, v, v, v],
        out_specs=(v, v, v, hbm, hbm, hbm, hbm),
        scratch_shapes=[
            pltpu.VMEM((rows // tile, tile, cols), F32), pltpu.VMEM((cols, count), BF16), pltpu.VMEM((cols, count), BF16),
            vmem(16, count), vmem(rows, count), vmem(count, count), vmem(2, cells, count),
            vmem(rows // cells, cells, count), vmem(RING, cells, count), vmem(RING, cells, count),
            vmem(2, cells // 2, count), vmem(2, cells, count),
            vmem(count, count), vmem(half, count), vmem(2, 3, p1, half), vmem(2, 3, p2, half), vmem(2, 3, 8, 128),
            vmem(count, count),
            pltpu.SemaphoreType.DMA((rows // tile,)), pltpu.SemaphoreType.DMA((120,)), pltpu.SemaphoreType.DMA((120,))],
        compiler_params=pltpu.CompilerParams(vmem_limit_bytes=62 << 20, collective_id=0, has_side_effects=True),
        cost_estimate=pl.CostEstimate(flops=12 * 10**9, bytes_accessed=20 << 20, transcendentals=0),
    )(p, velf, vels, oi, oj, noise, wl)


def cell_weights(vel_first, vel_second, start, lines):
    first = lax.dynamic_slice_in_dim(vel_first, start, lines, 0)
    second = lax.dynamic_slice_in_dim(vel_second, start, lines, 0)
    line = lax.broadcasted_iota(jnp.int32, second.shape, 0) + start
    at = lax.broadcasted_iota(jnp.int32, second.shape, 1)
    ends = second.shape[1] - 1
    return [w.reshape(-1) for w in (
        jnp.where(line == ends, 0.0, dispersion - 0.5 * first),
        jnp.where(line == 0, 0.0, dispersion + 0.5 * first),
        jnp.where(at == ends, 0.0, dispersion - 0.5 * second),
        jnp.where(at == 0, 0.0, dispersion + 0.5 * second))]


def body(prior, vel_first, vel_second, obs_cell, obs_noise):
    rows, cols = prior.shape
    cells = vel_first.shape[0]
    row_lines, col_lines = rows // cells, cols // cells
    row_place, col_place = lax.axis_index("row"), lax.axis_index("col")
    wl = jnp.stack(cell_weights(vel_first, vel_second, row_place * row_lines, row_lines), axis=1)
    wr = jnp.stack(cell_weights(vel_first, vel_second, col_place * col_lines, col_lines), axis=0)
    oi, oj = obs_cell[:, 0][None], obs_cell[:, 1][None]
    s_inv, g_rows, g_cols, top, bot, lo, hi = exchange(prior, vel_first, vel_second, oi, oj, obs_noise[None], wl)
    field = forecast(wl, wr, top, prior, bot, lo, hi, cells)
    return finish(field, g_rows, s_inv, g_cols, tile=512)


def solution(mesh):
    placed = (P("row", "col"), P(), P(), P(), P())
    return jax.shard_map(body, mesh=mesh, in_specs=placed, out_specs=P("row", "col"), check_vma=False)
```

```python
import functools
import jax
import jax.numpy as jnp
from jax import lax
from jax.experimental import pallas as pl
from jax.experimental.pallas import tpu as pltpu
from jax.sharding import PartitionSpec as P

HI = lax.Precision.HIGHEST
F32, BF16 = jnp.float32, jnp.bfloat16
dispersion = 0.125
centre_weight = 1.0 - 4.0 * dispersion
interp_weights = (0.42, 0.28, 0.18, 0.12)

def split(x):
    hi = x.astype(BF16)
    return hi, (x - hi.astype(F32)).astype(BF16)

def dot3(a, b, dims):
    (ah, al), (bh, bl) = a, b
    dg = functools.partial(lax.dot_general, dimension_numbers=(dims, ((), ())), preferred_element_type=F32)
    return dg(ah, bh) + (dg(ah, bl) + dg(al, bh))

def observed_weights(velf_ref, vels_ref, oi, oj):
    cells, count = velf_ref.shape[0], oi.shape[1]
    cid = lax.broadcasted_iota(jnp.int32, (cells, count), 0)
    w = {}
    def add(di, dj, v):
        w[di, dj] = w[di, dj] + v if (di, dj) in w else v
    for a in (0, 1):
        pick = jnp.where(cid == oi + a, 1.0, 0.0).astype(F32)
        by_j = [lax.dot_general(v[...], pick, (((0,), (0,)), ((), ())), precision=HI, preferred_element_type=F32)
                for v in (velf_ref, vels_ref)]
        for b in (0, 1):
            here = cid == oj + b
            vf, vs = [jnp.sum(jnp.where(here, x, 0.0), axis=0, keepdims=True) for x in by_j]
            h = interp_weights[2 * a + b]
            add(a, b, jnp.full_like(vf, h * centre_weight))
            add(a + 1, b, h * (dispersion - 0.5 * vf))
            add(a - 1, b, h * (dispersion + 0.5 * vf))
            add(a, b + 1, h * (dispersion - 0.5 * vs))
            add(a, b - 1, h * (dispersion + 0.5 * vs))
    return w

def line_weights(w, oi, oj, line, cells):
    count = oi.shape[1]
    jid = lax.broadcasted_iota(jnp.int32, (cells, count), 0)
    out = jnp.zeros((cells, count), F32)
    for dj in (-1, 0, 1, 2):
        row = jnp.zeros((1, count), F32)
        for di in (-1, 0, 1, 2):
            if (di, dj) in w:
                row = row + jnp.where(oi + di == line, w[di, dj], 0.0)
        out = jnp.where(jid == oj + dj, row, out)
    return out


def observed_panel(first_row, first_col, fetch, velf_ref, vels_ref, obs_ref, ext, t_ext, s_ref, ch, cl, wsc):
    cells = velf_ref.shape[0]
    lines, cols = ext.shape[0] - 2, ext.shape[2] - 2 * cells
    w = observed_weights(velf_ref, vels_ref, obs_ref[0:1, :], obs_ref[1:2, :])
    keys = sorted(w)
    for n, key in enumerate(keys):
        wsc[n:n + 1, :] = w[key]

    def at_line(line):
        table = {key: wsc[n:n + 1, :] for n, key in enumerate(keys)}
        return line_weights(table, obs_ref[0:1, :], obs_ref[1:2, :], line, cells)

    def build(l, _):
        at = pl.ds(pl.multiple_of(l * cells, cells), cells)
        ch[at, :], cl[at, :] = split(at_line(first_col + l))
        return 0
    lax.fori_loop(0, cols // cells, build, 0)
    s_ref[...] = jnp.zeros_like(s_ref)
    take = 2

    def run(n, _):
        for m in range(take):
            fetch(n * take + m).wait()
        at = pl.ds(1 + n * take, take)
        p = ext[at, :, cells:cells + cols].reshape(take * cells, cols)
        t = dot3(split(p), (ch[...], cl[...]), ((1,), (0,)))
        t_ext[at] = t.reshape(take, cells, t.shape[1])
        c = jnp.concatenate([at_line(first_row + n * take + m) for m in range(take)], axis=0)
        s_ref[...] += dot3(split(c), split(t), ((0,), (0,)))
        return 0
    lax.fori_loop(0, lines // take, run, 0)


def left_sweep(prev, mid, nxt, w):
    cells = mid.shape[0]
    up = pltpu.roll(mid, cells - 1, 0)
    down = pltpu.roll(mid, 1, 0)
    return centre_weight * mid + w[0] * nxt + w[1] * prev + w[2] * up + w[3] * down


def stencil_tables(velf_ref, vels_ref, first_row, first_col, wl, wr):
    cells = velf_ref.shape[0]
    by_first, by_second = velf_ref[...].T, vels_ref[...].T
    rid = lax.broadcasted_iota(jnp.int32, (cells, cells), 0)
    cid = lax.broadcasted_iota(jnp.int32, (cells, cells), 1)
    ends = cells - 1

    def row_line(l, _):
        line = first_row + l
        here = cid == line
        a, b = [jnp.broadcast_to(jnp.sum(jnp.where(here, v, 0.0), axis=1, keepdims=True), (cells, cells))
                for v in (by_first, by_second)]
        wl[l, 0] = jnp.where(line == ends, 0.0, dispersion - 0.5 * a)
        wl[l, 1] = jnp.where(line == 0, 0.0, dispersion + 0.5 * a)
        wl[l, 2] = jnp.where(rid == ends, 0.0, dispersion - 0.5 * b)
        wl[l, 3] = jnp.where(rid == 0, 0.0, dispersion + 0.5 * b)
        return 0
    lax.fori_loop(0, wl.shape[0], row_line, 0)

    def col_line(l, _):
        line = first_col + l
        a, b = velf_ref[pl.ds(line, 1), :], vels_ref[pl.ds(line, 1), :]
        lane = cid[:1]
        wr[l, 0:1, :] = jnp.where(line == ends, 0.0, dispersion - 0.5 * a)
        wr[l, 1:2, :] = jnp.where(line == 0, 0.0, dispersion + 0.5 * a)
        wr[l, 2:3, :] = jnp.where(lane == ends, 0.0, dispersion - 0.5 * b)
        wr[l, 3:4, :] = jnp.where(lane == 0, 0.0, dispersion + 0.5 * b)
        return 0
    lax.fori_loop(0, wr.shape[0], col_line, 0)


def forecast_line(i, ext, wl, wr, q_ref, f_ref):
    cells = ext.shape[1]
    spans = q_ref.shape[0]

    def rows_of(l):
        s = pl.ds(pl.multiple_of(l * cells, cells), cells)
        w = [wl[i, m] for m in range(4)]
        q_ref[l] = left_sweep(ext[i, :, s], ext[i + 1, :, s], ext[i + 2, :, s], w)

    def cols_of(l):
        s = pl.ds(pl.multiple_of(l * cells, cells), cells)
        mid = q_ref[l + 1]
        f_ref[i, :, s] = (centre_weight * mid + wr[l, 0:1, :] * q_ref[l + 2] + wr[l, 1:2, :] * q_ref[l]
                          + wr[l, 2:3, :] * pltpu.roll(mid, cells - 1, 1) + wr[l, 3:4, :] * pltpu.roll(mid, 1, 1))

    def pair(f):
        def run(n, _):
            f(2 * n)
            f(2 * n + 1)
            return 0
        return run
    lax.fori_loop(0, spans // 2, pair(rows_of), 0)
    lax.fori_loop(0, spans // 2 - 1, pair(cols_of), 0)


def fin_kernel(f_ref, g_ref, s_ref, gc_ref, o_ref, wh, wlo):
    @pl.when(pl.program_id(0) == 0)
    def _():
        w = jnp.dot(g_ref[...], s_ref[...], precision=HI, preferred_element_type=F32)
        h, l = split(w)
        wh[...] = h
        wlo[...] = l
    o_ref[...] = f_ref[...] - dot3((wh[...], wlo[...]), split(gc_ref[...]), ((1,), (1,)))

def finish(f, g, s, gc, tile=256):
    rows, cols = f.shape
    count = s.shape[0]
    whole = lambda x: pl.BlockSpec(x.shape, lambda n: (0, 0), pipeline_mode=pl.Buffered(1))
    return pl.pallas_call(fin_kernel, grid=(cols // tile,),
        out_shape=jax.ShapeDtypeStruct((rows, cols), F32),
        in_specs=[pl.BlockSpec((rows, tile), lambda n: (0, n)), whole(g), whole(s), pl.BlockSpec((tile, count), lambda n: (n, 0))],
        out_specs=pl.BlockSpec((rows, tile), lambda n: (0, n)),
        scratch_shapes=[pltpu.VMEM((rows, count), BF16), pltpu.VMEM((rows, count), BF16)],
        compiler_params=pltpu.CompilerParams(vmem_limit_bytes=40 << 20),
        cost_estimate=pl.CostEstimate(flops=8 * 10**9, bytes_accessed=24 << 20, transcendentals=0),
    )(f, g, s, gc)


def invert_in(s_ref, noise_ref, o_ref, hooks, block=128, parts=4):
    n = s_ref.shape[0]
    s = s_ref[...]
    rid = lax.broadcasted_iota(jnp.int32, (n, n), 0)
    cid = lax.broadcasted_iota(jnp.int32, (n, n), 1)
    o_ref[...] = 0.5 * (s + s.T) + jnp.where(rid == cid, noise_ref[...], 0.0)
    nb = n // block
    for k in range(nb):
        own = slice(k * block, (k + 1) * block)
        a = o_ref[own, own]
        for part in range(parts):
            for hook in hooks.get((k, part), ()):
                hook()
            a = pivot(a, range(part * block // parts, (part + 1) * block // parts, 4))
        panel = jnp.dot(a, o_ref[own, :], precision=HI, preferred_element_type=F32)
        col = o_ref[:, own]
        for j in range(nb):
            here = slice(j * block, (j + 1) * block)
            r = a if j == k else panel[:, here]
            upd = jnp.dot(col, r, precision=HI, preferred_element_type=F32)
            o_ref[:, here] = -upd if j == k else o_ref[:, here] - upd
            o_ref[own, here] = r


def pivot(a, steps):
    rid = lax.broadcasted_iota(jnp.int32, a.shape, 0)
    cid = lax.broadcasted_iota(jnp.int32, a.shape, 1)
    lane = cid[:1]
    four = range(4)
    for k in steps:
        col = [jnp.broadcast_to(a[:, k + j:k + j + 1], a.shape) for j in four]
        p = {(i, j): col[j][k + i:k + i + 1, :] for j in four for i in range(j + 1)}
        inside = (lane >= k) & (lane < k + 4)
        row = [jnp.where(inside, jnp.where(lane == k + j, 1.0, 0.0), a[k + j:k + j + 1, :]) for j in four]
        det = 1.0 / (p[0, 0] * p[1, 1] - p[0, 1] * p[0, 1])
        a00, a01, a11 = p[1, 1] * det, -p[0, 1] * det, p[0, 0] * det
        x00, x01 = a00 * p[0, 2] + a01 * p[1, 2], a00 * p[0, 3] + a01 * p[1, 3]
        x10, x11 = a01 * p[0, 2] + a11 * p[1, 2], a01 * p[0, 3] + a11 * p[1, 3]
        s22 = p[2, 2] - (p[0, 2] * x00 + p[1, 2] * x10)
        s23 = p[2, 3] - (p[0, 2] * x01 + p[1, 2] * x11)
        s33 = p[3, 3] - (p[0, 3] * x01 + p[1, 3] * x11)
        u0, u1 = a00 * row[0] + a01 * row[1], a01 * row[0] + a11 * row[1]
        v2 = row[2] - (x00 * row[0] + x10 * row[1])
        v3 = row[3] - (x01 * row[0] + x11 * row[1])
        det = 1.0 / (s22 * s33 - s23 * s23)
        r2, r3 = (s33 * v2 - s23 * v3) * det, (s22 * v3 - s23 * v2) * det
        r0, r1 = u0 - (x00 * r2 + x01 * r3), u1 - (x10 * r2 + x11 * r3)
        base = jnp.where((cid >= k) & (cid < k + 4), 0.0, a)
        a = base - ((col[0] * r0 + col[1] * r1) + (col[2] * r2 + col[3] * r3))
        for j, r in enumerate((r0, r1, r2, r3)):
            a = jnp.where(rid == k + j, r, a)
    return a


MESH = pl.DeviceIdType.MESH
RING = 4


def exchange_kernel(p_hbm, velf_ref, vels_ref, obs_ref, noise_ref,
                    sinv_ref, grow_ref, gcol_ref, f_hbm,
                    ext, ch, cl, wsc, wl, wr, q_ref, f_ref, t_ext, s_ref, gp, rg, gs, ry, rl,
                    s_acc, r0, r1, r2, r3, s_out, in_sems, out_sems, send_sems, recv_sems):
    lines, cells, cols = p_hbm.shape
    count = obs_ref.shape[1]
    row, col = lax.axis_index("row"), lax.axis_index("col")
    row_count, col_count = lax.axis_size("row"), lax.axis_size("col")
    x, z = row // RING, row % RING
    y, core = col // 2, col % 2
    col_lines = cols // cells
    inner = pl.ds(cells, cols)

    def fetch(n):
        return pltpu.make_async_copy(p_hbm.at[n], ext.at[n + 1, :, inner], in_sems.at[n])

    for n in range(lines):
        fetch(n).start()

    def step(v, d):
        return (v + d + RING) % RING

    def chip(dx=0, dy=0, dz=0):
        return (step(x, dx) * RING + step(z, dz), step(y, dy) * 2 + core)

    partner = (row, col + 1 - 2 * core)
    twin_row = y * RING + 2 * core + z % 2
    twin_col = 2 * x + z // 2
    twin = (twin_row, twin_col)
    alone = (twin_row == row) & (twin_col == col)
    up, down = (row + 1) % row_count, (row + row_count - 1) % row_count
    right, left = (col + 1) % col_count, (col + col_count - 1) % col_count

    barrier = pltpu.get_barrier_semaphore()
    greeted = [partner, (up, col), (down, col), (row, right), (row, left),
               (up, right), (up, left), (down, right), (down, left)]
    greeted += [chip(dx=d) for d in (1, 2, 3)] + [chip(dy=d) for d in (1, 2, 3)] + [chip(dz=d) for d in (1, 2, 3)]
    for peer in greeted:
        pl.semaphore_signal(barrier, inc=1, device_id=peer, device_id_type=MESH)

    @pl.when(jnp.logical_not(alone))
    def _():
        pl.semaphore_signal(barrier, inc=1, device_id=twin, device_id_type=MESH)
    pl.semaphore_wait(barrier, len(greeted) + 1 - alone.astype(jnp.int32))

    used, sent = {}, []

    def slot(key):
        if key not in used:
            used[key] = len(used)
        return used[key]

    def copy(key, src, dst, peer):
        n = slot(key)
        return pltpu.make_async_remote_copy(src_ref=src, dst_ref=dst, send_sem=send_sems.at[n], recv_sem=recv_sems.at[n],
                                            device_id=peer, device_id_type=MESH)

    def send(key, src, dst, peer):
        c = copy(key, src, dst, peer)
        c.start()
        sent.append(c)

    def arrive(key, dst, peer):
        copy(key, dst, dst, peer).wait_recv()

    low, high = pl.ds(0, cells), pl.ds(cols + cells, cells)
    head, tail = pl.ds(0, cells), pl.ds(cols - cells, cells)
    top, bot = 0, lines + 1
    late = cols // 4
    block = pl.ds(1, lines)
    halo = [
        ("p_right", p_hbm.at[:, :, tail], ext.at[block, :, low], (row, right), (row, left)),
        ("p_left", p_hbm.at[:, :, head], ext.at[block, :, high], (row, left), (row, right)),
        ("p_up_right", p_hbm.at[lines - 1, :, tail], ext.at[top, :, low], (up, right), (down, left)),
        ("p_up_left", p_hbm.at[lines - 1, :, head], ext.at[top, :, high], (up, left), (down, right)),
        ("p_down_right", p_hbm.at[0, :, tail], ext.at[bot, :, low], (down, right), (up, left)),
        ("p_down_left", p_hbm.at[0, :, head], ext.at[bot, :, high], (down, left), (up, right)),
        ("p_up", p_hbm.at[lines - 1, :, pl.ds(late, cols - late)], ext.at[top, :, pl.ds(cells + late, cols - late)],
         (up, col), (down, col)),
        ("p_down", p_hbm.at[0, :, pl.ds(late, cols - late)], ext.at[bot, :, pl.ds(cells + late, cols - late)],
         (down, col), (up, col)),
        ("p_up_late", p_hbm.at[lines - 1, :, pl.ds(0, late)], ext.at[top, :, pl.ds(cells, late)], (up, col), (down, col)),
        ("p_down_late", p_hbm.at[0, :, pl.ds(0, late)], ext.at[bot, :, pl.ds(cells, late)], (down, col), (up, col)),
    ]
    for key, src, dst, to, _ in halo[:8]:
        send(key, src, dst, to)

    first_row, first_col = row * lines, col * col_lines
    stencil_tables(velf_ref, vels_ref, first_row, first_col, wl, wr)
    observed_panel(first_row, first_col, fetch, velf_ref, vels_ref, obs_ref, ext, t_ext, s_ref, ch, cl, wsc)

    def forecast_lines(start, stop):
        def one(i, _):
            forecast_line(i, ext, wl, wr, q_ref, f_ref)
            pltpu.make_async_copy(f_ref.at[i], f_hbm.at[i], out_sems.at[i]).start()
            return 0
        lax.fori_loop(start, stop, one, 0)

    send("t_up", t_ext.at[lines], t_ext.at[top], (up, col))
    send("t_down", t_ext.at[1], t_ext.at[bot], (down, col))
    half = count // 2
    mine = pl.multiple_of(core * half, half)
    other = pl.multiple_of(half - core * half, half)
    send("s_core", s_ref.at[pl.ds(other, half), :], r0.at[:, :], partner)
    for key, src, dst, to, _ in halo[8:]:
        send(key, src, dst, to)
    for key, _, dst, _, frm in halo[:2]:
        arrive(key, dst, frm)
    forecast_lines(1, 2)
    arrive("s_core", r0.at[:, :], partner)
    s_acc[pl.ds(mine, half), :] = s_ref[pl.ds(mine, half), :] + r0[...]

    wide = count // 2
    p1, p2 = half // RING, half // RING**2
    order = (("x", "y"), ("y", "x"))
    pos = {"x": x, "y": y, "z": z}

    def at1(a, i):
        return (pl.ds(pl.multiple_of(mine + i * p1, 8), p1), pl.ds(a * wide, wide))

    def at2(a, i, j):
        return (pl.ds(pl.multiple_of(mine + i * p1 + j * p2, 8), p2), pl.ds(a * wide, wide))

    def hop(axis, d):
        return chip(**{"d" + axis: d})

    def reduce_start(name, slots, place, axes):
        for a in (0, 1):
            for d in (1, 2, 3):
                axis = axes[a]
                send((name, a, d), s_acc.at[place(a, step(pos[axis], d))], slots.at[a, d - 1], hop(axis, d))

    def reduce_end(name, slots, place, axes):
        for a in (0, 1):
            for d in (1, 2, 3):
                arrive((name, a, d), slots.at[a, d - 1], hop(axes[a], -d))
            here = place(a, pos[axes[a]])
            s_acc[here] = (s_acc[here] + slots[a, 0]) + (slots[a, 1] + slots[a, 2])

    def gather_start(name, place, axes):
        for a in (0, 1):
            here = place(a, pos[axes[a]])
            for d in (1, 2, 3):
                send((name, a, d), s_out.at[here], s_out.at[here], hop(axes[a], d))

    def gather_end(name, place, axes):
        for a in (0, 1):
            for d in (1, 2, 3):
                there = place(a, step(pos[axes[a]], -d))
                arrive((name, a, d), s_out.at[there], hop(axes[a], -d))

    axes1, axes2 = [o[0] for o in order], [o[1] for o in order]
    own1 = [pos[a] for a in axes1]
    own2 = [pos[a] for a in axes2]
    place1 = at1
    place2 = lambda a, j: at2(a, own1[a], j)

    reduce_start("s1", r1, place1, axes1)

    forecast_lines(2, 4)

    arrive("t_up", t_ext.at[top], (down, col))
    arrive("t_down", t_ext.at[bot], (up, col))

    def sweep_line(l, _):
        w = [wl[l, m] for m in range(4)]
        for b in range(count // cells):
            s = slice(b * cells, (b + 1) * cells)
            gp[l, :, s] = left_sweep(t_ext[l, :, s], t_ext[l + 1, :, s], t_ext[l + 2, :, s], w)
        return 0
    lax.fori_loop(0, lines, sweep_line, 0)
    for q in range(RING):
        send(("g_core", q), gp.at[2 * q + 1 - core], rg.at[q], partner)

    reduce_end("s1", r1, place1, axes1)
    reduce_start("s2", r2, place2, axes2)

    for q in range(RING):
        arrive(("g_core", q), rg.at[q], partner)
        gs[q] = gp[2 * q + core] + rg[q]
    h = cells // 2
    first, second = pl.ds(0, h), pl.ds(h, h)
    far, nxt_y, prv_y = step(y, 2), step(y, 1), step(y, -1)
    send("g_far_up", gs.at[far, first], ry.at[0], chip(dy=1))
    send("g_far_down", gs.at[far, second], ry.at[1], chip(dy=-1))

    forecast_lines(4, 5)
    reduce_end("s2", r2, place2, axes2)
    for a in (0, 1):
        piece2 = s_acc.at[place2(a, own2[a])]
        for d in (1, 2, 3):
            send(("s3", a, d), piece2, r3.at[a, z], chip(dz=d))
        r3[a, z] = s_acc[place2(a, own2[a])]

    arrive("g_far_up", ry.at[0], chip(dy=-1))
    arrive("g_far_down", ry.at[1], chip(dy=1))
    gs[nxt_y, first] = gs[nxt_y, first] + ry[0]
    gs[prv_y, second] = gs[prv_y, second] + ry[1]
    send("g_up", gs.at[nxt_y], rl.at[0], chip(dy=1))
    send("g_down", gs.at[prv_y], rl.at[1], chip(dy=-1))

    forecast_lines(5, 6)
    for a in (0, 1):
        for d in (1, 2, 3):
            arrive(("s3", a, d), r3.at[a, step(z, -d)], chip(dz=-d))
        s_out[place2(a, own2[a])] = (r3[a, 0] + r3[a, 1]) + (r3[a, 2] + r3[a, 3])
    gather_start("a2", place2, axes2)
    forecast_lines(6, 7)
    gather_end("a2", place2, axes2)
    gather_start("a1", place1, axes1)

    arrive("g_up", rl.at[0], chip(dy=-1))
    arrive("g_down", rl.at[1], chip(dy=1))

    def line_at(c, lo=0, n=cells):
        return (pl.ds(pl.multiple_of(c * cells + lo, 8), n), slice(None))

    own = line_at(col)
    grow_ref[own] = (gs[y] + rl[0]) + rl[1]

    def col_line(xx, zz, lo=0, n=cells):
        return line_at(8 * (zz % 2) + 2 * xx + zz // 2, lo, n)

    landing = col_line(x, z)
    away = line_at(8 * (row % 2) + col)
    twin_copy = copy("twin", grow_ref.at[own], gcol_ref.at[away], twin)

    @pl.when(alone)
    def _():
        gcol_ref[landing] = grow_ref[own]

    @pl.when(jnp.logical_not(alone))
    def _():
        twin_copy.start()

    send("y_up", grow_ref.at[own], grow_ref.at[own], chip(dy=1))
    send("y_down", grow_ref.at[own], grow_ref.at[own], chip(dy=-1))
    send(("c", 0), grow_ref.at[own], grow_ref.at[own], partner)

    for key, _, dst, _, frm in halo[2:]:
        arrive(key, dst, frm)
    forecast_lines(0, 1)
    forecast_lines(7, 8)
    gather_end("a1", place1, axes1)
    whole = (pl.ds(mine, half), slice(None))
    send("s_back", s_out.at[whole], s_out.at[whole], partner)

    def c_of(d):
        return 2 * step(y, d) + core

    def twin_landed():
        @pl.when(jnp.logical_not(alone))
        def _():
            arrive("twin", gcol_ref.at[landing], twin)

    lows = (0, h)
    rings = (("x", "z"), ("z", "x"))

    def piece(a, d0, d1, lo=0, n=h):
        dx, dz = (d0, d1) if a == 0 else (d1, d0)
        return gcol_ref.at[col_line(step(x, dx), step(z, dz), lows[a] + lo, n)]

    def turn(a, level, d):
        return hop(rings[a][level], d)

    def p1():
        twin_landed()
        for a in (0, 1):
            for d in (1, -1):
                send(("q1", a, d), piece(a, 0, 0), piece(a, 0, 0), turn(a, 0, d))
        for a in (0, 1):
            for d in (1, -1):
                send(("q2", a, 0, d), piece(a, 0, 0), piece(a, 0, 0), turn(a, 1, d))
        arrive("y_up", grow_ref.at[line_at(c_of(-1))], chip(dy=-1))
        arrive("y_down", grow_ref.at[line_at(c_of(1))], chip(dy=1))
        send("y_far_up", grow_ref.at[line_at(c_of(-1), 0, h)], grow_ref.at[line_at(c_of(-1), 0, h)], chip(dy=1))
        send("y_far_down", grow_ref.at[line_at(c_of(1), h, h)], grow_ref.at[line_at(c_of(1), h, h)], chip(dy=-1))
        for d in (-1, 1):
            send(("c", d), grow_ref.at[line_at(c_of(d))], grow_ref.at[line_at(c_of(d))], partner)

    def p2():
        for a in (0, 1):
            for d in (1, -1):
                arrive(("q1", a, d), piece(a, -d, 0), turn(a, 0, -d))
                lo = 0 if d == 1 else h // 2
                send(("q1r", a, d), piece(a, -d, 0, lo, h // 2), piece(a, -d, 0, lo, h // 2), turn(a, 0, d))
        for a in (0, 1):
            for k in (-1, 1):
                for d in (1, -1):
                    send(("q2", a, k, d), piece(a, k, 0), piece(a, k, 0), turn(a, 1, d))

    def p3():
        for a in (0, 1):
            for d in (1, -1):
                lo = 0 if d == 1 else h // 2
                arrive(("q1r", a, d), piece(a, -2 * d, 0, lo, h // 2), turn(a, 0, -d))
            for d in (1, -1):
                send(("q2", a, 2, d), piece(a, 2, 0), piece(a, 2, 0), turn(a, 1, d))

    def relay(a, k, d):
        arrive(("q2", a, k, d), piece(a, k, -d), turn(a, 1, -d))
        if (k in (0, -1)) == (d == 1):
            send(("q2r", a, k), piece(a, k, -d), piece(a, k, -d), turn(a, 1, d))

    def relays(*ks):
        def run():
            for k in ks:
                for a in (0, 1):
                    for d in (1, -1):
                        relay(a, k, d)
        return run

    def p4():
        arrive("y_far_up", grow_ref.at[line_at(c_of(-2), 0, h)], chip(dy=-1))
        arrive("y_far_down", grow_ref.at[line_at(c_of(2), h, h)], chip(dy=1))
        send(("c", 2), grow_ref.at[line_at(c_of(2))], grow_ref.at[line_at(c_of(2))], partner)

    hooks = {(0, 2): [p1], (1, 1): [p2], (1, 3): [p3, relays(0)], (2, 2): [p4, relays(-1, 1)], (3, 1): [relays(2)]}

    arrive("s_back", s_out.at[pl.ds(other, half), :], partner)
    invert_in(s_out, noise_ref, sinv_ref, hooks)

    for d in (0, -1, 1, 2):
        there = line_at(2 * step(y, d) + 1 - core)
        arrive(("c", d), grow_ref.at[there], partner)
    for a in (0, 1):
        for k in (0, -1, 1, 2):
            d = 1 if k in (0, -1) else -1
            arrive(("q2r", a, k), piece(a, k, -2 * d), turn(a, 1, -d))
    for c in sent:
        c.wait_send()
    for n in range(lines):
        pltpu.make_async_copy(f_ref.at[n], f_hbm.at[n], out_sems.at[n]).wait()

    @pl.when(jnp.logical_not(alone))
    def _():
        twin_copy.wait_send()


def exchange(p, velf, vels, obs, noise):
    rows, cols = p.shape
    count, cells = obs.shape[1], velf.shape[0]
    lines = rows // cells
    half = count // 2
    p1, p2 = half // RING, half // RING**2
    v = pl.BlockSpec(memory_space=pltpu.VMEM)
    hbm = pl.BlockSpec(memory_space=pl.ANY)
    shape = lambda *s: jax.ShapeDtypeStruct(s, F32)
    vmem = lambda *s: pltpu.VMEM(s, F32)
    return pl.pallas_call(exchange_kernel,
        out_shape=(shape(count, count), shape(rows, count), shape(cols, count), shape(lines, cells, cols)),
        in_specs=[hbm, v, v, v, v],
        out_specs=(v, v, v, hbm),
        scratch_shapes=[
            vmem(lines + 2, cells, cols + 2 * cells), pltpu.VMEM((cols, count), BF16), pltpu.VMEM((cols, count), BF16),
            vmem(16, count), vmem(lines, 4, cells, cells), vmem(cols // cells, 8, cells), vmem(cols // cells + 2, cells, cells),
            vmem(lines, cells, cols), vmem(lines + 2, cells, count), vmem(count, count),
            vmem(lines, cells, count), vmem(RING, cells, count), vmem(RING, cells, count),
            vmem(2, cells // 2, count), vmem(2, cells, count),
            vmem(count, count), vmem(half, count), vmem(2, 3, p1, half), vmem(2, 3, p2, half), vmem(2, RING, p2, half),
            vmem(count, count),
            pltpu.SemaphoreType.DMA((lines,)), pltpu.SemaphoreType.DMA((lines,)),
            pltpu.SemaphoreType.DMA((100,)), pltpu.SemaphoreType.DMA((100,))],
        compiler_params=pltpu.CompilerParams(vmem_limit_bytes=62 << 20, collective_id=0, has_side_effects=True),
        cost_estimate=pl.CostEstimate(flops=12 * 10**9, bytes_accessed=28 << 20, transcendentals=0),
    )(p.reshape(lines, cells, cols), velf, vels, obs, noise)


def body(prior, vel_first, vel_second, obs_cell, obs_noise):
    s_inv, g_rows, g_cols, field = exchange(prior, vel_first, vel_second, obs_cell.T, obs_noise[None])
    return finish(field.reshape(prior.shape), g_rows, s_inv, g_cols, tile=512)


def solution(mesh):
    placed = (P("row", "col"), P(), P(), P(), P())
    return jax.shard_map(body, mesh=mesh, in_specs=placed, out_specs=P("row", "col"), check_vma=False)
```

```python
import functools
import jax
import jax.numpy as jnp
from jax import lax
from jax.experimental import pallas as pl
from jax.experimental.pallas import tpu as pltpu
from jax.sharding import PartitionSpec as P

HI = lax.Precision.HIGHEST
F32, BF16 = jnp.float32, jnp.bfloat16
dispersion = 0.125
centre_weight = 1.0 - 4.0 * dispersion
interp_weights = (0.42, 0.28, 0.18, 0.12)

def split(x):
    hi = x.astype(BF16)
    return hi, (x - hi.astype(F32)).astype(BF16)

def dot3(a, b, dims):
    (ah, al), (bh, bl) = a, b
    dg = functools.partial(lax.dot_general, dimension_numbers=(dims, ((), ())), preferred_element_type=F32)
    return dg(ah, bh) + (dg(ah, bl) + dg(al, bh))

def observed_weights(velf_ref, vels_ref, oi, oj):
    cells, count = velf_ref.shape[0], oi.shape[1]
    cid = lax.broadcasted_iota(jnp.int32, (cells, count), 0)
    w = {}
    def add(di, dj, v):
        w[di, dj] = w[di, dj] + v if (di, dj) in w else v
    for a in (0, 1):
        pick = jnp.where(cid == oi + a, 1.0, 0.0).astype(F32)
        by_j = [lax.dot_general(v[...], pick, (((0,), (0,)), ((), ())), precision=HI, preferred_element_type=F32)
                for v in (velf_ref, vels_ref)]
        for b in (0, 1):
            here = cid == oj + b
            vf, vs = [jnp.sum(jnp.where(here, x, 0.0), axis=0, keepdims=True) for x in by_j]
            h = interp_weights[2 * a + b]
            add(a, b, jnp.full_like(vf, h * centre_weight))
            add(a + 1, b, h * (dispersion - 0.5 * vf))
            add(a - 1, b, h * (dispersion + 0.5 * vf))
            add(a, b + 1, h * (dispersion - 0.5 * vs))
            add(a, b - 1, h * (dispersion + 0.5 * vs))
    return w

def line_weights(w, oi, oj, line, cells):
    count = oi.shape[1]
    jid = lax.broadcasted_iota(jnp.int32, (cells, count), 0)
    out = jnp.zeros((cells, count), F32)
    for dj in (-1, 0, 1, 2):
        row = jnp.zeros((1, count), F32)
        for di in (-1, 0, 1, 2):
            if (di, dj) in w:
                row = row + jnp.where(oi + di == line, w[di, dj], 0.0)
        out = jnp.where(jid == oj + dj, row, out)
    return out


def observed_panel(first_row, first_col, fetch, velf_ref, vels_ref, obs_ref, ext, t_ext, s_ref, ch, cl, wsc, send_edges):
    cells = velf_ref.shape[0]
    lines, cols = ext.shape[0] - 2, ext.shape[2] - 2 * cells
    w = observed_weights(velf_ref, vels_ref, obs_ref[0:1, :], obs_ref[1:2, :])
    keys = sorted(w)
    for n, key in enumerate(keys):
        wsc[n:n + 1, :] = w[key]

    def at_line(line):
        table = {key: wsc[n:n + 1, :] for n, key in enumerate(keys)}
        return line_weights(table, obs_ref[0:1, :], obs_ref[1:2, :], line, cells)

    def build(l, _):
        at = pl.ds(pl.multiple_of(l * cells, cells), cells)
        ch[at, :], cl[at, :] = split(at_line(first_col + l))
        return 0
    lax.fori_loop(0, cols // cells, build, 0)
    s_ref[...] = jnp.zeros_like(s_ref)
    take = 2

    def run(n, _):
        for m in range(take):
            fetch(n * take + m).wait()
        at = pl.ds(1 + n * take, take)
        p = ext[at, :, cells:cells + cols].reshape(take * cells, cols)
        t = dot3(split(p), (ch[...], cl[...]), ((1,), (0,)))
        t_ext[at] = t.reshape(take, cells, t.shape[1])
        c = jnp.concatenate([at_line(first_row + n * take + m) for m in range(take)], axis=0)
        s_ref[...] += dot3(split(c), split(t), ((0,), (0,)))
        return 0
    last = lines // take - 1
    lax.fori_loop(0, 2, lambda n, _: run(n * last, _), 0)
    send_edges()
    lax.fori_loop(1, last, run, 0)


def left_sweep(prev, mid, nxt, w):
    cells = mid.shape[0]
    up = pltpu.roll(mid, cells - 1, 0)
    down = pltpu.roll(mid, 1, 0)
    return centre_weight * mid + w[0] * nxt + w[1] * prev + w[2] * up + w[3] * down


def stencil_tables(velf_ref, vels_ref, first_row, first_col, wl, wr):
    cells = velf_ref.shape[0]
    by_first, by_second = velf_ref[...].T, vels_ref[...].T
    rid = lax.broadcasted_iota(jnp.int32, (cells, cells), 0)
    cid = lax.broadcasted_iota(jnp.int32, (cells, cells), 1)
    ends = cells - 1

    def row_line(l, _):
        line = first_row + l
        here = cid == line
        a, b = [jnp.broadcast_to(jnp.sum(jnp.where(here, v, 0.0), axis=1, keepdims=True), (cells, cells))
                for v in (by_first, by_second)]
        wl[l, 0] = jnp.where(line == ends, 0.0, dispersion - 0.5 * a)
        wl[l, 1] = jnp.where(line == 0, 0.0, dispersion + 0.5 * a)
        wl[l, 2] = jnp.where(rid == ends, 0.0, dispersion - 0.5 * b)
        wl[l, 3] = jnp.where(rid == 0, 0.0, dispersion + 0.5 * b)
        return 0
    lax.fori_loop(0, wl.shape[0], row_line, 0)

    def col_line(l, _):
        line = first_col + l
        a, b = velf_ref[pl.ds(line, 1), :], vels_ref[pl.ds(line, 1), :]
        lane = cid[:1]
        wr[l, 0:1, :] = jnp.where(line == ends, 0.0, dispersion - 0.5 * a)
        wr[l, 1:2, :] = jnp.where(line == 0, 0.0, dispersion + 0.5 * a)
        wr[l, 2:3, :] = jnp.where(lane == ends, 0.0, dispersion - 0.5 * b)
        wr[l, 3:4, :] = jnp.where(lane == 0, 0.0, dispersion + 0.5 * b)
        return 0
    lax.fori_loop(0, wr.shape[0], col_line, 0)


def forecast_line(i, ext, wl, wr, q_ref, f_ref):
    cells = ext.shape[1]
    spans = q_ref.shape[0]

    def rows_of(l):
        s = pl.ds(pl.multiple_of(l * cells, cells), cells)
        w = [wl[i, m] for m in range(4)]
        q_ref[l] = left_sweep(ext[i, :, s], ext[i + 1, :, s], ext[i + 2, :, s], w)

    def cols_of(l):
        s = pl.ds(pl.multiple_of(l * cells, cells), cells)
        mid = q_ref[l + 1]
        f_ref[i, :, s] = (centre_weight * mid + wr[l, 0:1, :] * q_ref[l + 2] + wr[l, 1:2, :] * q_ref[l]
                          + wr[l, 2:3, :] * pltpu.roll(mid, cells - 1, 1) + wr[l, 3:4, :] * pltpu.roll(mid, 1, 1))

    def pair(f):
        def run(n, _):
            f(2 * n)
            f(2 * n + 1)
            return 0
        return run
    lax.fori_loop(0, spans // 2, pair(rows_of), 0)
    lax.fori_loop(0, spans // 2 - 1, pair(cols_of), 0)


def fin_kernel(f_ref, wh_ref, wlo_ref, gc_ref, o_ref):
    o_ref[...] = f_ref[...] - dot3((wh_ref[...], wlo_ref[...]), split(gc_ref[...]), ((1,), (1,)))


def finish(f, wh, wlo, gc, tile=512):
    rows, cols = f.shape
    count = gc.shape[1]
    whole = lambda x: pl.BlockSpec(x.shape, lambda n: (0, 0), pipeline_mode=pl.Buffered(1))
    return pl.pallas_call(fin_kernel, grid=(cols // tile,),
        out_shape=jax.ShapeDtypeStruct((rows, cols), F32),
        in_specs=[pl.BlockSpec((rows, tile), lambda n: (0, n)), whole(wh), whole(wlo), pl.BlockSpec((tile, count), lambda n: (n, 0))],
        out_specs=pl.BlockSpec((rows, tile), lambda n: (0, n)),
        compiler_params=pltpu.CompilerParams(vmem_limit_bytes=62 << 20),
        cost_estimate=pl.CostEstimate(flops=8 * 10**9, bytes_accessed=24 << 20, transcendentals=0),
    )(f, wh, wlo, gc)


def invert_in(s_ref, noise_ref, o_ref, hooks, block=128, parts=4):
    n = s_ref.shape[0]
    s = s_ref[...]
    rid = lax.broadcasted_iota(jnp.int32, (n, n), 0)
    cid = lax.broadcasted_iota(jnp.int32, (n, n), 1)
    o_ref[...] = 0.5 * (s + s.T) + jnp.where(rid == cid, noise_ref[...], 0.0)
    nb = n // block
    for k in range(nb):
        own = slice(k * block, (k + 1) * block)
        a = o_ref[own, own]
        for part in range(parts):
            for hook in hooks.get((k, part), ()):
                hook()
            a = pivot(a, range(part * block // parts, (part + 1) * block // parts, 4))
        panel = jnp.dot(a, o_ref[own, :], precision=HI, preferred_element_type=F32)
        col = o_ref[:, own]
        for j in range(nb):
            here = slice(j * block, (j + 1) * block)
            r = a if j == k else panel[:, here]
            upd = jnp.dot(col, r, precision=HI, preferred_element_type=F32)
            o_ref[:, here] = -upd if j == k else o_ref[:, here] - upd
            o_ref[own, here] = r


def pivot(a, steps):
    rid = lax.broadcasted_iota(jnp.int32, a.shape, 0)
    cid = lax.broadcasted_iota(jnp.int32, a.shape, 1)
    lane = cid[:1]
    four = range(4)
    for k in steps:
        col = [jnp.broadcast_to(a[:, k + j:k + j + 1], a.shape) for j in four]
        p = {(i, j): col[j][k + i:k + i + 1, :] for j in four for i in range(j + 1)}
        inside = (lane >= k) & (lane < k + 4)
        row = [jnp.where(inside, jnp.where(lane == k + j, 1.0, 0.0), a[k + j:k + j + 1, :]) for j in four]
        det = 1.0 / (p[0, 0] * p[1, 1] - p[0, 1] * p[0, 1])
        a00, a01, a11 = p[1, 1] * det, -p[0, 1] * det, p[0, 0] * det
        x00, x01 = a00 * p[0, 2] + a01 * p[1, 2], a00 * p[0, 3] + a01 * p[1, 3]
        x10, x11 = a01 * p[0, 2] + a11 * p[1, 2], a01 * p[0, 3] + a11 * p[1, 3]
        s22 = p[2, 2] - (p[0, 2] * x00 + p[1, 2] * x10)
        s23 = p[2, 3] - (p[0, 2] * x01 + p[1, 2] * x11)
        s33 = p[3, 3] - (p[0, 3] * x01 + p[1, 3] * x11)
        u0, u1 = a00 * row[0] + a01 * row[1], a01 * row[0] + a11 * row[1]
        v2 = row[2] - (x00 * row[0] + x10 * row[1])
        v3 = row[3] - (x01 * row[0] + x11 * row[1])
        det = 1.0 / (s22 * s33 - s23 * s23)
        r2, r3 = (s33 * v2 - s23 * v3) * det, (s22 * v3 - s23 * v2) * det
        r0, r1 = u0 - (x00 * r2 + x01 * r3), u1 - (x10 * r2 + x11 * r3)
        base = jnp.where((cid >= k) & (cid < k + 4), 0.0, a)
        a = base - ((col[0] * r0 + col[1] * r1) + (col[2] * r2 + col[3] * r3))
        for j, r in enumerate((r0, r1, r2, r3)):
            a = jnp.where(rid == k + j, r, a)
    return a


MESH = pl.DeviceIdType.MESH
RING = 4


def exchange_kernel(p_hbm, velf_ref, vels_ref, obs_ref, noise_ref,
                    wh_ref, wlo_ref, gcol_ref, f_hbm,
                    ext, ch, cl, wsc, wl, wr, q_ref, f_ref, t_ext, s_ref, gp, rg, gs, ry, rl,
                    s_acc, r0, r1, r2, r3, s_out, sinv_ref, grow_ref, in_sems, out_sems, twin_sem, send_sems, recv_sems):
    lines, cells, cols = p_hbm.shape
    count = obs_ref.shape[1]
    row, col = lax.axis_index("row"), lax.axis_index("col")
    row_count, col_count = lax.axis_size("row"), lax.axis_size("col")
    x, z = row // RING, row % RING
    y, core = col // 2, col % 2
    col_lines = cols // cells
    inner = pl.ds(cells, cols)

    def fetch(n):
        return pltpu.make_async_copy(p_hbm.at[n], ext.at[n + 1, :, inner], in_sems.at[n])

    for n in range(lines):
        fetch(n).start()

    def step(v, d):
        return (v + d + RING) % RING

    def chip(dx=0, dy=0, dz=0):
        return (step(x, dx) * RING + step(z, dz), step(y, dy) * 2 + core)

    partner = (row, col + 1 - 2 * core)
    twin_row = y * RING + 2 * core + z % 2
    twin_col = 2 * x + z // 2
    twin = (twin_row, twin_col)
    alone = (twin_row == row) & (twin_col == col)
    up, down = (row + 1) % row_count, (row + row_count - 1) % row_count
    right, left = (col + 1) % col_count, (col + col_count - 1) % col_count

    barrier = pltpu.get_barrier_semaphore()
    greeted = [partner, (up, col), (down, col), (row, right), (row, left),
               (up, right), (up, left), (down, right), (down, left)]
    greeted += [chip(dx=d) for d in (1, 2, 3)] + [chip(dy=d) for d in (1, 2, 3)] + [chip(dz=d) for d in (1, 2, 3)]
    for peer in greeted:
        pl.semaphore_signal(barrier, inc=1, device_id=peer, device_id_type=MESH)

    @pl.when(jnp.logical_not(alone))
    def _():
        pl.semaphore_signal(barrier, inc=1, device_id=twin, device_id_type=MESH)
    pl.semaphore_wait(barrier, len(greeted) + 1 - alone.astype(jnp.int32))

    used, sent = {}, []

    def slot(key):
        if key not in used:
            used[key] = len(used)
        return used[key]

    def copy(key, src, dst, peer):
        n = slot(key)
        return pltpu.make_async_remote_copy(src_ref=src, dst_ref=dst, send_sem=send_sems.at[n], recv_sem=recv_sems.at[n],
                                            device_id=peer, device_id_type=MESH)

    def send(key, src, dst, peer):
        c = copy(key, src, dst, peer)
        c.start()
        sent.append(c)

    def arrive(key, dst, peer):
        copy(key, dst, dst, peer).wait_recv()

    low, high = pl.ds(0, cells), pl.ds(cols + cells, cells)
    head, tail = pl.ds(0, cells), pl.ds(cols - cells, cells)
    top, bot = 0, lines + 1
    bounds = [cols * n // 16 for n in (0, 6, 8, 9, 10, 16)]
    block = pl.ds(1, lines)
    halo = [
        ("p_right", p_hbm.at[:, :, tail], ext.at[block, :, low], (row, right), (row, left)),
        ("p_left", p_hbm.at[:, :, head], ext.at[block, :, high], (row, left), (row, right)),
        ("p_up_right", p_hbm.at[lines - 1, :, tail], ext.at[top, :, low], (up, right), (down, left)),
        ("p_up_left", p_hbm.at[lines - 1, :, head], ext.at[top, :, high], (up, left), (down, right)),
        ("p_down_right", p_hbm.at[0, :, tail], ext.at[bot, :, low], (down, right), (up, left)),
        ("p_down_left", p_hbm.at[0, :, head], ext.at[bot, :, high], (down, left), (up, right)),
    ]
    strips = []
    for n, (lo, hi) in enumerate(zip(bounds[:-1], bounds[1:])):
        src, dst = pl.ds(lo, hi - lo), pl.ds(cells + lo, hi - lo)
        strips.append([
            (("p_up", n), p_hbm.at[lines - 1, :, src], ext.at[top, :, dst], (up, col), (down, col)),
            (("p_down", n), p_hbm.at[0, :, src], ext.at[bot, :, dst], (down, col), (up, col))])

    def send_strip(n):
        for key, src, dst, to, _ in strips[n]:
            send(key, src, dst, to)

    for key, src, dst, to, _ in halo:
        send(key, src, dst, to)
    send_strip(0)

    first_row, first_col = row * lines, col * col_lines
    stencil_tables(velf_ref, vels_ref, first_row, first_col, wl, wr)
    def send_edges():
        send("t_up", t_ext.at[lines], t_ext.at[top], (up, col))
        send("t_down", t_ext.at[1], t_ext.at[bot], (down, col))

    observed_panel(first_row, first_col, fetch, velf_ref, vels_ref, obs_ref, ext, t_ext, s_ref, ch, cl, wsc, send_edges)

    def forecast_lines(start, stop):
        def one(i, _):
            forecast_line(i, ext, wl, wr, q_ref, f_ref)
            pltpu.make_async_copy(f_ref.at[i], f_hbm.at[i], out_sems.at[i]).start()
            return 0
        lax.fori_loop(start, stop, one, 0)

    half = count // 2
    mine = pl.multiple_of(core * half, half)
    other = pl.multiple_of(half - core * half, half)
    send("s_core", s_ref.at[pl.ds(other, half), :], r0.at[:, :], partner)
    for key, _, dst, _, frm in halo[:2]:
        arrive(key, dst, frm)
    forecast_lines(1, 2)
    arrive("s_core", r0.at[:, :], partner)
    s_acc[pl.ds(mine, half), :] = s_ref[pl.ds(mine, half), :] + r0[...]

    wide = count // 2
    p1, p2 = half // RING, half // RING**2
    order = (("x", "y"), ("y", "x"))
    pos = {"x": x, "y": y, "z": z}

    def at1(a, i):
        return (pl.ds(pl.multiple_of(mine + i * p1, 8), p1), pl.ds(a * wide, wide))

    def at2(a, i, j):
        return (pl.ds(pl.multiple_of(mine + i * p1 + j * p2, 8), p2), pl.ds(a * wide, wide))

    def hop(axis, d):
        return chip(**{"d" + axis: d})

    def reduce_start(name, slots, place, axes):
        for a in (0, 1):
            for d in (1, 2, 3):
                axis = axes[a]
                send((name, a, d), s_acc.at[place(a, step(pos[axis], d))], slots.at[a, d - 1], hop(axis, d))

    def reduce_end(name, slots, place, axes):
        for a in (0, 1):
            for d in (1, 2, 3):
                arrive((name, a, d), slots.at[a, d - 1], hop(axes[a], -d))
            here = place(a, pos[axes[a]])
            s_acc[here] = (s_acc[here] + slots[a, 0]) + (slots[a, 1] + slots[a, 2])

    def gather_start(name, place, axes):
        for a in (0, 1):
            here = place(a, pos[axes[a]])
            for d in (1, 2, 3):
                send((name, a, d), s_out.at[here], s_out.at[here], hop(axes[a], d))

    def gather_end(name, place, axes):
        for a in (0, 1):
            for d in (1, 2, 3):
                there = place(a, step(pos[axes[a]], -d))
                arrive((name, a, d), s_out.at[there], hop(axes[a], -d))

    axes1, axes2 = [o[0] for o in order], [o[1] for o in order]
    own1 = [pos[a] for a in axes1]
    own2 = [pos[a] for a in axes2]
    place1 = at1
    place2 = lambda a, j: at2(a, own1[a], j)

    reduce_start("s1", r1, place1, axes1)
    send_strip(1)


    arrive("t_up", t_ext.at[top], (down, col))
    arrive("t_down", t_ext.at[bot], (up, col))

    def sweep_line(l, _):
        w = [wl[l, m] for m in range(4)]
        for b in range(count // cells):
            s = slice(b * cells, (b + 1) * cells)
            gp[l, :, s] = left_sweep(t_ext[l, :, s], t_ext[l + 1, :, s], t_ext[l + 2, :, s], w)
        return 0
    lax.fori_loop(0, lines, sweep_line, 0)
    for q in range(RING):
        send(("g_core", q), gp.at[2 * q + 1 - core], rg.at[q], partner)
    forecast_lines(2, 3)

    reduce_end("s1", r1, place1, axes1)
    reduce_start("s2", r2, place2, axes2)
    send_strip(2)

    for q in range(RING):
        arrive(("g_core", q), rg.at[q], partner)
        gs[q] = gp[2 * q + core] + rg[q]
    h = cells // 2
    first, second = pl.ds(0, h), pl.ds(h, h)
    far, nxt_y, prv_y = step(y, 2), step(y, 1), step(y, -1)
    send("g_far_up", gs.at[far, first], ry.at[0], chip(dy=1))
    send("g_far_down", gs.at[far, second], ry.at[1], chip(dy=-1))

    forecast_lines(3, 4)
    reduce_end("s2", r2, place2, axes2)
    for a in (0, 1):
        piece2 = s_acc.at[place2(a, own2[a])]
        for d in (1, 2, 3):
            send(("s3", a, d), piece2, r3.at[a, z], chip(dz=d))
        r3[a, z] = s_acc[place2(a, own2[a])]

    forecast_lines(4, 5)
    for a in (0, 1):
        for d in (1, 2, 3):
            arrive(("s3", a, d), r3.at[a, step(z, -d)], chip(dz=-d))
        s_out[place2(a, own2[a])] = (r3[a, 0] + r3[a, 1]) + (r3[a, 2] + r3[a, 3])
    gather_start("a2", place2, axes2)
    arrive("g_far_up", ry.at[0], chip(dy=-1))
    arrive("g_far_down", ry.at[1], chip(dy=1))
    gs[nxt_y, first] = gs[nxt_y, first] + ry[0]
    gs[prv_y, second] = gs[prv_y, second] + ry[1]
    send("g_up", gs.at[nxt_y], rl.at[0], chip(dy=1))
    send("g_down", gs.at[prv_y], rl.at[1], chip(dy=-1))
    send_strip(3)
    forecast_lines(5, 6)
    gather_end("a2", place2, axes2)
    gather_start("a1", place1, axes1)
    send_strip(4)
    forecast_lines(6, 7)

    arrive("g_up", rl.at[0], chip(dy=-1))
    arrive("g_down", rl.at[1], chip(dy=1))

    def line_at(c, lo=0, n=cells):
        return (pl.ds(pl.multiple_of(c * cells + lo, 8), n), slice(None))

    own = line_at(col)
    grow_ref[own] = (gs[y] + rl[0]) + rl[1]

    def col_line(xx, zz, lo=0, n=cells):
        return line_at(8 * (zz % 2) + 2 * xx + zz // 2, lo, n)

    landing = col_line(x, z)
    away = line_at(8 * (row % 2) + col)
    twin_copy = copy("twin", grow_ref.at[own], gcol_ref.at[away], twin)

    @pl.when(alone)
    def _():
        pltpu.make_async_copy(grow_ref.at[own], gcol_ref.at[landing], twin_sem).start()

    @pl.when(jnp.logical_not(alone))
    def _():
        twin_copy.start()

    send("y_up", grow_ref.at[own], grow_ref.at[own], chip(dy=1))
    send("y_down", grow_ref.at[own], grow_ref.at[own], chip(dy=-1))
    send(("c", 0), grow_ref.at[own], grow_ref.at[own], partner)

    gather_end("a1", place1, axes1)
    whole = (pl.ds(mine, half), slice(None))
    send("s_back", s_out.at[whole], s_out.at[whole], partner)

    def c_of(d):
        return 2 * step(y, d) + core

    def twin_landed():
        @pl.when(jnp.logical_not(alone))
        def _():
            arrive("twin", gcol_ref.at[landing], twin)

        @pl.when(alone)
        def _():
            pltpu.make_async_copy(grow_ref.at[own], gcol_ref.at[landing], twin_sem).wait()

    lows = (0, h)
    rings = (("x", "z"), ("z", "x"))

    def piece(a, d0, d1, lo=0, n=h):
        dx, dz = (d0, d1) if a == 0 else (d1, d0)
        return gcol_ref.at[col_line(step(x, dx), step(z, dz), lows[a] + lo, n)]

    def turn(a, level, d):
        return hop(rings[a][level], d)

    def p1():
        twin_landed()
        for a in (0, 1):
            for d in (1, -1):
                send(("q1", a, d), piece(a, 0, 0), piece(a, 0, 0), turn(a, 0, d))
        for a in (0, 1):
            for d in (1, -1):
                send(("q2", a, 0, d), piece(a, 0, 0), piece(a, 0, 0), turn(a, 1, d))
        arrive("y_up", grow_ref.at[line_at(c_of(-1))], chip(dy=-1))
        arrive("y_down", grow_ref.at[line_at(c_of(1))], chip(dy=1))
        send("y_far_up", grow_ref.at[line_at(c_of(-1), 0, h)], grow_ref.at[line_at(c_of(-1), 0, h)], chip(dy=1))
        send("y_far_down", grow_ref.at[line_at(c_of(1), h, h)], grow_ref.at[line_at(c_of(1), h, h)], chip(dy=-1))
        for d in (-1, 1):
            send(("c", d), grow_ref.at[line_at(c_of(d))], grow_ref.at[line_at(c_of(d))], partner)

    def p2():
        for a in (0, 1):
            for d in (1, -1):
                arrive(("q1", a, d), piece(a, -d, 0), turn(a, 0, -d))
                lo = 0 if d == 1 else h // 2
                send(("q1r", a, d), piece(a, -d, 0, lo, h // 2), piece(a, -d, 0, lo, h // 2), turn(a, 0, d))
        for a in (0, 1):
            for k in (-1, 1):
                for d in (1, -1):
                    send(("q2", a, k, d), piece(a, k, 0), piece(a, k, 0), turn(a, 1, d))

    def p3():
        for a in (0, 1):
            for d in (1, -1):
                lo = 0 if d == 1 else h // 2
                arrive(("q1r", a, d), piece(a, -2 * d, 0, lo, h // 2), turn(a, 0, -d))
            for d in (1, -1):
                send(("q2", a, 2, d), piece(a, 2, 0), piece(a, 2, 0), turn(a, 1, d))

    def relay(a, k, d):
        arrive(("q2", a, k, d), piece(a, k, -d), turn(a, 1, -d))
        if (k in (0, -1)) == (d == 1):
            send(("q2r", a, k), piece(a, k, -d), piece(a, k, -d), turn(a, 1, d))

    def relays(*ks):
        def run():
            for k in ks:
                for a in (0, 1):
                    for d in (1, -1):
                        relay(a, k, d)
        return run

    def p4():
        arrive("y_far_up", grow_ref.at[line_at(c_of(-2), 0, h)], chip(dy=-1))
        arrive("y_far_down", grow_ref.at[line_at(c_of(2), h, h)], chip(dy=1))
        send(("c", 2), grow_ref.at[line_at(c_of(2))], grow_ref.at[line_at(c_of(2))], partner)

    def edge_lines():
        for key, _, dst, _, frm in halo[2:] + sum(strips, []):
            arrive(key, dst, frm)
        forecast_lines(0, 1)
        forecast_lines(lines - 1, lines)

    hooks = {(0, 2): [p1], (1, 1): [edge_lines, p2], (1, 3): [p3, relays(0)], (2, 2): [p4, relays(-1, 1)], (3, 1): [relays(2)]}

    arrive("s_back", s_out.at[pl.ds(other, half), :], partner)
    invert_in(s_out, noise_ref, sinv_ref, hooks)

    for d in (0, -1, 1, 2):
        there = line_at(2 * step(y, d) + 1 - core)
        arrive(("c", d), grow_ref.at[there], partner)

    def update_rows(n, _):
        at = pl.ds(pl.multiple_of(n * 2 * cells, 2 * cells), 2 * cells)
        w = jnp.dot(grow_ref[at, :], sinv_ref[...], precision=HI, preferred_element_type=F32)
        wh_ref[at, :], wlo_ref[at, :] = split(w)
        return 0
    lax.fori_loop(0, lines // 2, update_rows, 0)
    for a in (0, 1):
        for k in (0, -1, 1, 2):
            d = 1 if k in (0, -1) else -1
            arrive(("q2r", a, k), piece(a, k, -2 * d), turn(a, 1, -d))
    for c in sent:
        c.wait_send()
    for n in range(lines):
        pltpu.make_async_copy(f_ref.at[n], f_hbm.at[n], out_sems.at[n]).wait()

    @pl.when(jnp.logical_not(alone))
    def _():
        twin_copy.wait_send()


def exchange(p, velf, vels, obs, noise):
    rows, cols = p.shape
    count, cells = obs.shape[1], velf.shape[0]
    lines = rows // cells
    half = count // 2
    p1, p2 = half // RING, half // RING**2
    v = pl.BlockSpec(memory_space=pltpu.VMEM)
    hbm = pl.BlockSpec(memory_space=pl.ANY)
    shape = lambda *s: jax.ShapeDtypeStruct(s, F32)
    vmem = lambda *s: pltpu.VMEM(s, F32)
    return pl.pallas_call(exchange_kernel,
        out_shape=(jax.ShapeDtypeStruct((rows, count), BF16), jax.ShapeDtypeStruct((rows, count), BF16), shape(cols, count),
                   shape(lines, cells, cols)),
        in_specs=[hbm, v, v, v, v],
        out_specs=(v, v, hbm, hbm),
        scratch_shapes=[
            vmem(lines + 2, cells, cols + 2 * cells), pltpu.VMEM((cols, count), BF16), pltpu.VMEM((cols, count), BF16),
            vmem(16, count), vmem(lines, 4, cells, cells), vmem(cols // cells, 8, cells), vmem(cols // cells + 2, cells, cells),
            vmem(lines, cells, cols), vmem(lines + 2, cells, count), vmem(count, count),
            vmem(lines, cells, count), vmem(RING, cells, count), vmem(RING, cells, count),
            vmem(2, cells // 2, count), vmem(2, cells, count),
            vmem(count, count), vmem(half, count), vmem(2, 3, p1, half), vmem(2, 3, p2, half), vmem(2, RING, p2, half),
            vmem(count, count), vmem(count, count), vmem(rows, count),
            pltpu.SemaphoreType.DMA((lines,)), pltpu.SemaphoreType.DMA((lines,)), pltpu.SemaphoreType.DMA,
            pltpu.SemaphoreType.DMA((100,)), pltpu.SemaphoreType.DMA((100,))],
        compiler_params=pltpu.CompilerParams(vmem_limit_bytes=62 << 20, collective_id=0, has_side_effects=True),
        cost_estimate=pl.CostEstimate(flops=12 * 10**9, bytes_accessed=28 << 20, transcendentals=0),
    )(p.reshape(lines, cells, cols), velf, vels, obs, noise)


def body(prior, vel_first, vel_second, obs_cell, obs_noise):
    w_high, w_low, g_cols, field = exchange(prior, vel_first, vel_second, obs_cell.T, obs_noise[None])
    return finish(field.reshape(prior.shape), w_high, w_low, g_cols)


def solution(mesh):
    placed = (P("row", "col"), P(), P(), P(), P())
    return jax.shard_map(body, mesh=mesh, in_specs=placed, out_specs=P("row", "col"), check_vma=False)
```

```python
import functools
import jax
import jax.numpy as jnp
from jax import lax
from jax.experimental import pallas as pl
from jax.experimental.pallas import tpu as pltpu
from jax.sharding import PartitionSpec as P

HI = lax.Precision.HIGHEST
F32, BF16 = jnp.float32, jnp.bfloat16
dispersion = 0.125
centre_weight = 1.0 - 4.0 * dispersion
interp_weights = (0.42, 0.28, 0.18, 0.12)

def split(x):
    hi = x.astype(BF16)
    return hi, (x - hi.astype(F32)).astype(BF16)

def dot3(a, b, dims):
    (ah, al), (bh, bl) = a, b
    dg = functools.partial(lax.dot_general, dimension_numbers=(dims, ((), ())), preferred_element_type=F32)
    return dg(ah, bh) + (dg(ah, bl) + dg(al, bh))

def observed_weights(velf_ref, vels_ref, oi, oj):
    cells, count = velf_ref.shape[0], oi.shape[1]
    cid = lax.broadcasted_iota(jnp.int32, (cells, count), 0)
    w = {}
    def add(di, dj, v):
        w[di, dj] = w[di, dj] + v if (di, dj) in w else v
    for a in (0, 1):
        pick = jnp.where(cid == oi + a, 1.0, 0.0).astype(F32)
        by_j = [lax.dot_general(v[...], pick, (((0,), (0,)), ((), ())), precision=HI, preferred_element_type=F32)
                for v in (velf_ref, vels_ref)]
        for b in (0, 1):
            here = cid == oj + b
            vf, vs = [jnp.sum(jnp.where(here, x, 0.0), axis=0, keepdims=True) for x in by_j]
            h = interp_weights[2 * a + b]
            add(a, b, jnp.full_like(vf, h * centre_weight))
            add(a + 1, b, h * (dispersion - 0.5 * vf))
            add(a - 1, b, h * (dispersion + 0.5 * vf))
            add(a, b + 1, h * (dispersion - 0.5 * vs))
            add(a, b - 1, h * (dispersion + 0.5 * vs))
    return w

def line_weights(w, oi, oj, line, cells):
    count = oi.shape[1]
    jid = lax.broadcasted_iota(jnp.int32, (cells, count), 0)
    out = jnp.zeros((cells, count), F32)
    for dj in (-1, 0, 1, 2):
        row = jnp.zeros((1, count), F32)
        for di in (-1, 0, 1, 2):
            if (di, dj) in w:
                row = row + jnp.where(oi + di == line, w[di, dj], 0.0)
        out = jnp.where(jid == oj + dj, row, out)
    return out


def observed_panel(first_row, first_col, fetch, velf_ref, vels_ref, obs_ref, ext, t_ext, s_ref, ch, cl, wsc, send_edges):
    cells = velf_ref.shape[0]
    lines, cols = ext.shape[0] - 2, ext.shape[2] - 2 * cells
    w = observed_weights(velf_ref, vels_ref, obs_ref[0:1, :], obs_ref[1:2, :])
    keys = sorted(w)
    for n, key in enumerate(keys):
        wsc[n:n + 1, :] = w[key]

    def at_line(line):
        table = {key: wsc[n:n + 1, :] for n, key in enumerate(keys)}
        return line_weights(table, obs_ref[0:1, :], obs_ref[1:2, :], line, cells)

    def build(l, _):
        at = pl.ds(pl.multiple_of(l * cells, cells), cells)
        ch[at, :], cl[at, :] = split(at_line(first_col + l))
        return 0
    lax.fori_loop(0, cols // cells, build, 0)
    s_ref[...] = jnp.zeros_like(s_ref)
    take = 2

    def run(n, _):
        for m in range(take):
            fetch(n * take + m).wait()
        at = pl.ds(1 + n * take, take)
        p = ext[at, :, cells:cells + cols].reshape(take * cells, cols)
        t = dot3(split(p), (ch[...], cl[...]), ((1,), (0,)))
        t_ext[at] = t.reshape(take, cells, t.shape[1])
        c = jnp.concatenate([at_line(first_row + n * take + m) for m in range(take)], axis=0)
        s_ref[...] += dot3(split(c), split(t), ((0,), (0,)))
        return 0
    last = lines // take - 1
    lax.fori_loop(0, 2, lambda n, _: run(n * last, _), 0)
    send_edges()
    lax.fori_loop(1, last, run, 0)


def left_sweep(prev, mid, nxt, w):
    cells = mid.shape[0]
    up = pltpu.roll(mid, cells - 1, 0)
    down = pltpu.roll(mid, 1, 0)
    return centre_weight * mid + w[0] * nxt + w[1] * prev + w[2] * up + w[3] * down


def stencil_tables(velf_ref, vels_ref, first_row, first_col, wl, wr):
    cells = velf_ref.shape[0]
    by_first, by_second = velf_ref[...].T, vels_ref[...].T
    rid = lax.broadcasted_iota(jnp.int32, (cells, cells), 0)
    cid = lax.broadcasted_iota(jnp.int32, (cells, cells), 1)
    ends = cells - 1

    def row_line(l, _):
        line = first_row + l
        here = cid == line
        a, b = [jnp.broadcast_to(jnp.sum(jnp.where(here, v, 0.0), axis=1, keepdims=True), (cells, cells))
                for v in (by_first, by_second)]
        wl[l, 0] = jnp.where(line == ends, 0.0, dispersion - 0.5 * a)
        wl[l, 1] = jnp.where(line == 0, 0.0, dispersion + 0.5 * a)
        wl[l, 2] = jnp.where(rid == ends, 0.0, dispersion - 0.5 * b)
        wl[l, 3] = jnp.where(rid == 0, 0.0, dispersion + 0.5 * b)
        return 0
    lax.fori_loop(0, wl.shape[0], row_line, 0)

    def col_line(l, _):
        line = first_col + l
        a, b = velf_ref[pl.ds(line, 1), :], vels_ref[pl.ds(line, 1), :]
        lane = cid[:1]
        wr[l, 0:1, :] = jnp.where(line == ends, 0.0, dispersion - 0.5 * a)
        wr[l, 1:2, :] = jnp.where(line == 0, 0.0, dispersion + 0.5 * a)
        wr[l, 2:3, :] = jnp.where(lane == ends, 0.0, dispersion - 0.5 * b)
        wr[l, 3:4, :] = jnp.where(lane == 0, 0.0, dispersion + 0.5 * b)
        return 0
    lax.fori_loop(0, wr.shape[0], col_line, 0)


def forecast_line(i, ext, wl, wr, q_ref, f_ref):
    cells = ext.shape[1]
    spans = q_ref.shape[0]

    def rows_of(l):
        s = pl.ds(pl.multiple_of(l * cells, cells), cells)
        w = [wl[i, m] for m in range(4)]
        q_ref[l] = left_sweep(ext[i, :, s], ext[i + 1, :, s], ext[i + 2, :, s], w)

    def cols_of(l):
        s = pl.ds(pl.multiple_of(l * cells, cells), cells)
        mid = q_ref[l + 1]
        f_ref[i, :, s] = (centre_weight * mid + wr[l, 0:1, :] * q_ref[l + 2] + wr[l, 1:2, :] * q_ref[l]
                          + wr[l, 2:3, :] * pltpu.roll(mid, cells - 1, 1) + wr[l, 3:4, :] * pltpu.roll(mid, 1, 1))

    def pair(f):
        def run(n, _):
            f(2 * n)
            f(2 * n + 1)
            return 0
        return run
    lax.fori_loop(0, spans // 2, pair(rows_of), 0)
    lax.fori_loop(0, spans // 2 - 1, pair(cols_of), 0)


def fin_kernel(f_ref, wh_ref, wlo_ref, gc_ref, o_ref):
    o_ref[...] = f_ref[...] - dot3((wh_ref[...], wlo_ref[...]), split(gc_ref[...]), ((1,), (1,)))


def finish(f, wh, wlo, gc, tile=512):
    rows, cols = f.shape
    count = gc.shape[1]
    whole = lambda x: pl.BlockSpec(x.shape, lambda n: (0, 0), pipeline_mode=pl.Buffered(1))
    return pl.pallas_call(fin_kernel, grid=(cols // tile,),
        out_shape=jax.ShapeDtypeStruct((rows, cols), F32),
        in_specs=[pl.BlockSpec((rows, tile), lambda n: (0, n)), whole(wh), whole(wlo), pl.BlockSpec((tile, count), lambda n: (n, 0))],
        out_specs=pl.BlockSpec((rows, tile), lambda n: (0, n)),
        compiler_params=pltpu.CompilerParams(vmem_limit_bytes=62 << 20),
        cost_estimate=pl.CostEstimate(flops=8 * 10**9, bytes_accessed=24 << 20, transcendentals=0),
    )(f, wh, wlo, gc)


def invert_in(s_ref, noise_ref, o_ref, hooks, block=128, parts=4):
    n = s_ref.shape[0]
    s = s_ref[...]
    rid = lax.broadcasted_iota(jnp.int32, (n, n), 0)
    cid = lax.broadcasted_iota(jnp.int32, (n, n), 1)
    o_ref[...] = 0.5 * (s + s.T) + jnp.where(rid == cid, noise_ref[...], 0.0)
    nb = n // block
    for k in range(nb):
        own = slice(k * block, (k + 1) * block)
        a = o_ref[own, own]
        for part in range(parts):
            for hook in hooks.get((k, part), ()):
                hook()
            a = pivot(a, range(part * block // parts, (part + 1) * block // parts, 4))
        panel = jnp.dot(a, o_ref[own, :], precision=HI, preferred_element_type=F32)
        col = o_ref[:, own]
        for j in range(nb):
            here = slice(j * block, (j + 1) * block)
            r = a if j == k else panel[:, here]
            upd = jnp.dot(col, r, precision=HI, preferred_element_type=F32)
            o_ref[:, here] = -upd if j == k else o_ref[:, here] - upd
            o_ref[own, here] = r
    for hook in hooks.get((nb, 0), ()):
        hook()


def pivot(a, steps):
    rid = lax.broadcasted_iota(jnp.int32, a.shape, 0)
    cid = lax.broadcasted_iota(jnp.int32, a.shape, 1)
    lane = cid[:1]
    four = range(4)
    for k in steps:
        col = [jnp.broadcast_to(a[:, k + j:k + j + 1], a.shape) for j in four]
        p = {(i, j): col[j][k + i:k + i + 1, :] for j in four for i in range(j + 1)}
        inside = (lane >= k) & (lane < k + 4)
        row = [jnp.where(inside, jnp.where(lane == k + j, 1.0, 0.0), a[k + j:k + j + 1, :]) for j in four]
        det = 1.0 / (p[0, 0] * p[1, 1] - p[0, 1] * p[0, 1])
        a00, a01, a11 = p[1, 1] * det, -p[0, 1] * det, p[0, 0] * det
        x00, x01 = a00 * p[0, 2] + a01 * p[1, 2], a00 * p[0, 3] + a01 * p[1, 3]
        x10, x11 = a01 * p[0, 2] + a11 * p[1, 2], a01 * p[0, 3] + a11 * p[1, 3]
        s22 = p[2, 2] - (p[0, 2] * x00 + p[1, 2] * x10)
        s23 = p[2, 3] - (p[0, 2] * x01 + p[1, 2] * x11)
        s33 = p[3, 3] - (p[0, 3] * x01 + p[1, 3] * x11)
        u0, u1 = a00 * row[0] + a01 * row[1], a01 * row[0] + a11 * row[1]
        v2 = row[2] - (x00 * row[0] + x10 * row[1])
        v3 = row[3] - (x01 * row[0] + x11 * row[1])
        det = 1.0 / (s22 * s33 - s23 * s23)
        r2, r3 = (s33 * v2 - s23 * v3) * det, (s22 * v3 - s23 * v2) * det
        r0, r1 = u0 - (x00 * r2 + x01 * r3), u1 - (x10 * r2 + x11 * r3)
        base = jnp.where((cid >= k) & (cid < k + 4), 0.0, a)
        a = base - ((col[0] * r0 + col[1] * r1) + (col[2] * r2 + col[3] * r3))
        for j, r in enumerate((r0, r1, r2, r3)):
            a = jnp.where(rid == k + j, r, a)
    return a


MESH = pl.DeviceIdType.MESH
RING = 4


def exchange_kernel(p_hbm, velf_ref, vels_ref, obs_ref, noise_ref,
                    wh_ref, wlo_ref, gcol_ref, f_hbm,
                    ext, ch, cl, wsc, wl, wr, q_ref, f_ref, t_ext, s_ref, gp, rg, gs, ry, rl,
                    s_acc, r0, r1, r2, r3, s_out, sinv_ref, grow_ref, in_sems, out_sems, twin_sem, send_sems, recv_sems):
    lines, cells, cols = p_hbm.shape
    count = obs_ref.shape[1]
    row, col = lax.axis_index("row"), lax.axis_index("col")
    row_count, col_count = lax.axis_size("row"), lax.axis_size("col")
    x, z = row // RING, row % RING
    y, core = col // 2, col % 2
    col_lines = cols // cells
    inner = pl.ds(cells, cols)

    def fetch(n):
        return pltpu.make_async_copy(p_hbm.at[n], ext.at[n + 1, :, inner], in_sems.at[n])

    for n in range(lines):
        fetch(n).start()

    def step(v, d):
        return (v + d + RING) % RING

    def chip(dx=0, dy=0, dz=0):
        return (step(x, dx) * RING + step(z, dz), step(y, dy) * 2 + core)

    partner = (row, col + 1 - 2 * core)
    twin_row = y * RING + 2 * core + z % 2
    twin_col = 2 * x + z // 2
    twin = (twin_row, twin_col)
    alone = (twin_row == row) & (twin_col == col)
    up, down = (row + 1) % row_count, (row + row_count - 1) % row_count
    right, left = (col + 1) % col_count, (col + col_count - 1) % col_count

    barrier = pltpu.get_barrier_semaphore()
    greeted = [partner, (up, col), (down, col), (row, right), (row, left),
               (up, right), (up, left), (down, right), (down, left)]
    greeted += [chip(dx=d) for d in (1, 2, 3)] + [chip(dy=d) for d in (1, 2, 3)] + [chip(dz=d) for d in (1, 2, 3)]
    for peer in greeted:
        pl.semaphore_signal(barrier, inc=1, device_id=peer, device_id_type=MESH)

    @pl.when(jnp.logical_not(alone))
    def _():
        pl.semaphore_signal(barrier, inc=1, device_id=twin, device_id_type=MESH)
    pl.semaphore_wait(barrier, len(greeted) + 1 - alone.astype(jnp.int32))

    used, sent = {}, []

    def slot(key):
        if key not in used:
            used[key] = len(used)
        return used[key]

    def copy(key, src, dst, peer):
        n = slot(key)
        return pltpu.make_async_remote_copy(src_ref=src, dst_ref=dst, send_sem=send_sems.at[n], recv_sem=recv_sems.at[n],
                                            device_id=peer, device_id_type=MESH)

    def send(key, src, dst, peer):
        c = copy(key, src, dst, peer)
        c.start()
        sent.append(c)

    def arrive(key, dst, peer):
        copy(key, dst, dst, peer).wait_recv()

    low, high = pl.ds(0, cells), pl.ds(cols + cells, cells)
    head, tail = pl.ds(0, cells), pl.ds(cols - cells, cells)
    top, bot = 0, lines + 1
    bounds = [cols * n // 16 for n in (0, 6, 8, 9, 10, 16)]
    block = pl.ds(1, lines)
    halo = [
        ("p_right", p_hbm.at[:, :, tail], ext.at[block, :, low], (row, right), (row, left)),
        ("p_left", p_hbm.at[:, :, head], ext.at[block, :, high], (row, left), (row, right)),
        ("p_up_right", p_hbm.at[lines - 1, :, tail], ext.at[top, :, low], (up, right), (down, left)),
        ("p_up_left", p_hbm.at[lines - 1, :, head], ext.at[top, :, high], (up, left), (down, right)),
        ("p_down_right", p_hbm.at[0, :, tail], ext.at[bot, :, low], (down, right), (up, left)),
        ("p_down_left", p_hbm.at[0, :, head], ext.at[bot, :, high], (down, left), (up, right)),
    ]
    strips = []
    for n, (lo, hi) in enumerate(zip(bounds[:-1], bounds[1:])):
        src, dst = pl.ds(lo, hi - lo), pl.ds(cells + lo, hi - lo)
        strips.append([
            (("p_up", n), p_hbm.at[lines - 1, :, src], ext.at[top, :, dst], (up, col), (down, col)),
            (("p_down", n), p_hbm.at[0, :, src], ext.at[bot, :, dst], (down, col), (up, col))])

    def send_strip(n):
        for key, src, dst, to, _ in strips[n]:
            send(key, src, dst, to)

    for key, src, dst, to, _ in halo:
        send(key, src, dst, to)
    send_strip(0)

    first_row, first_col = row * lines, col * col_lines
    stencil_tables(velf_ref, vels_ref, first_row, first_col, wl, wr)
    def send_edges():
        send("t_up", t_ext.at[lines], t_ext.at[top], (up, col))
        send("t_down", t_ext.at[1], t_ext.at[bot], (down, col))

    observed_panel(first_row, first_col, fetch, velf_ref, vels_ref, obs_ref, ext, t_ext, s_ref, ch, cl, wsc, send_edges)

    def forecast_lines(start, stop):
        def one(i, _):
            forecast_line(i, ext, wl, wr, q_ref, f_ref)
            pltpu.make_async_copy(f_ref.at[i], f_hbm.at[i], out_sems.at[i]).start()
            return 0
        lax.fori_loop(start, stop, one, 0)

    half = count // 2
    mine = pl.multiple_of(core * half, half)
    other = pl.multiple_of(half - core * half, half)
    send("s_core", s_ref.at[pl.ds(other, half), :], r0.at[:, :], partner)
    for key, _, dst, _, frm in halo[:2]:
        arrive(key, dst, frm)
    forecast_lines(1, 2)
    arrive("s_core", r0.at[:, :], partner)
    s_acc[pl.ds(mine, half), :] = s_ref[pl.ds(mine, half), :] + r0[...]

    wide = count // 2
    p1, p2 = half // RING, half // RING**2
    order = (("x", "y"), ("y", "x"))
    pos = {"x": x, "y": y, "z": z}

    def at1(a, i):
        return (pl.ds(pl.multiple_of(mine + i * p1, 8), p1), pl.ds(a * wide, wide))

    def at2(a, i, j):
        return (pl.ds(pl.multiple_of(mine + i * p1 + j * p2, 8), p2), pl.ds(a * wide, wide))

    def hop(axis, d):
        return chip(**{"d" + axis: d})

    def reduce_start(name, slots, place, axes):
        for a in (0, 1):
            for d in (1, 2, 3):
                axis = axes[a]
                send((name, a, d), s_acc.at[place(a, step(pos[axis], d))], slots.at[a, d - 1], hop(axis, d))

    def reduce_end(name, slots, place, axes):
        for a in (0, 1):
            for d in (1, 2, 3):
                arrive((name, a, d), slots.at[a, d - 1], hop(axes[a], -d))
            here = place(a, pos[axes[a]])
            s_acc[here] = (s_acc[here] + slots[a, 0]) + (slots[a, 1] + slots[a, 2])

    def gather_start(name, place, axes):
        for a in (0, 1):
            here = place(a, pos[axes[a]])
            for d in (1, 2, 3):
                send((name, a, d), s_out.at[here], s_out.at[here], hop(axes[a], d))

    def gather_end(name, place, axes):
        for a in (0, 1):
            for d in (1, 2, 3):
                there = place(a, step(pos[axes[a]], -d))
                arrive((name, a, d), s_out.at[there], hop(axes[a], -d))

    axes1, axes2 = [o[0] for o in order], [o[1] for o in order]
    own1 = [pos[a] for a in axes1]
    own2 = [pos[a] for a in axes2]
    place1 = at1
    place2 = lambda a, j: at2(a, own1[a], j)

    reduce_start("s1", r1, place1, axes1)
    send_strip(1)


    arrive("t_up", t_ext.at[top], (down, col))
    arrive("t_down", t_ext.at[bot], (up, col))

    def sweep_line(l, _):
        w = [wl[l, m] for m in range(4)]
        for b in range(count // cells):
            s = slice(b * cells, (b + 1) * cells)
            gp[l, :, s] = left_sweep(t_ext[l, :, s], t_ext[l + 1, :, s], t_ext[l + 2, :, s], w)
        return 0
    lax.fori_loop(0, lines, sweep_line, 0)
    for q in range(RING):
        send(("g_core", q), gp.at[2 * q + 1 - core], rg.at[q], partner)
    forecast_lines(2, 3)

    reduce_end("s1", r1, place1, axes1)
    reduce_start("s2", r2, place2, axes2)
    send_strip(2)

    for q in range(RING):
        arrive(("g_core", q), rg.at[q], partner)
        gs[q] = gp[2 * q + core] + rg[q]
    h = cells // 2
    first, second = pl.ds(0, h), pl.ds(h, h)
    far, nxt_y, prv_y = step(y, 2), step(y, 1), step(y, -1)
    send("g_far_up", gs.at[far, first], ry.at[0], chip(dy=1))
    send("g_far_down", gs.at[far, second], ry.at[1], chip(dy=-1))

    forecast_lines(3, 4)
    reduce_end("s2", r2, place2, axes2)
    for a in (0, 1):
        piece2 = s_acc.at[place2(a, own2[a])]
        for d in (1, 2, 3):
            send(("s3", a, d), piece2, r3.at[a, z], chip(dz=d))
        r3[a, z] = s_acc[place2(a, own2[a])]

    forecast_lines(4, 5)
    for a in (0, 1):
        for d in (1, 2, 3):
            arrive(("s3", a, d), r3.at[a, step(z, -d)], chip(dz=-d))
        s_out[place2(a, own2[a])] = (r3[a, 0] + r3[a, 1]) + (r3[a, 2] + r3[a, 3])
    gather_start("a2", place2, axes2)
    arrive("g_far_up", ry.at[0], chip(dy=-1))
    arrive("g_far_down", ry.at[1], chip(dy=1))
    gs[nxt_y, first] = gs[nxt_y, first] + ry[0]
    gs[prv_y, second] = gs[prv_y, second] + ry[1]
    send("g_up", gs.at[nxt_y], rl.at[0], chip(dy=1))
    send("g_down", gs.at[prv_y], rl.at[1], chip(dy=-1))
    send_strip(3)
    forecast_lines(5, 6)
    gather_end("a2", place2, axes2)
    gather_start("a1", place1, axes1)
    send_strip(4)
    forecast_lines(6, 7)

    arrive("g_up", rl.at[0], chip(dy=-1))
    arrive("g_down", rl.at[1], chip(dy=1))

    def line_at(c, lo=0, n=cells):
        return (pl.ds(pl.multiple_of(c * cells + lo, 8), n), slice(None))

    own = line_at(col)
    grow_ref[own] = (gs[y] + rl[0]) + rl[1]

    def col_line(xx, zz, lo=0, n=cells):
        return line_at(8 * (zz % 2) + 2 * xx + zz // 2, lo, n)

    landing = col_line(x, z)
    away = line_at(8 * (row % 2) + col)
    twin_copy = copy("twin", grow_ref.at[own], gcol_ref.at[away], twin)

    @pl.when(alone)
    def _():
        pltpu.make_async_copy(grow_ref.at[own], gcol_ref.at[landing], twin_sem).start()

    @pl.when(jnp.logical_not(alone))
    def _():
        twin_copy.start()

    send("y_up", grow_ref.at[own], grow_ref.at[own], chip(dy=1))
    send("y_down", grow_ref.at[own], grow_ref.at[own], chip(dy=-1))
    send(("c", 0), grow_ref.at[own], grow_ref.at[own], partner)

    gather_end("a1", place1, axes1)
    whole = (pl.ds(mine, half), slice(None))
    send("s_back", s_out.at[whole], s_out.at[whole], partner)

    def c_of(d):
        return 2 * step(y, d) + core

    def twin_landed():
        @pl.when(jnp.logical_not(alone))
        def _():
            arrive("twin", gcol_ref.at[landing], twin)

        @pl.when(alone)
        def _():
            pltpu.make_async_copy(grow_ref.at[own], gcol_ref.at[landing], twin_sem).wait()

    lows = (0, h)
    rings = (("x", "z"), ("z", "x"))

    def piece(a, d0, d1, lo=0, n=h):
        dx, dz = (d0, d1) if a == 0 else (d1, d0)
        return gcol_ref.at[col_line(step(x, dx), step(z, dz), lows[a] + lo, n)]

    def turn(a, level, d):
        return hop(rings[a][level], d)

    def p1():
        twin_landed()
        for a in (0, 1):
            for d in (1, -1):
                send(("q1", a, d), piece(a, 0, 0), piece(a, 0, 0), turn(a, 0, d))
        for a in (0, 1):
            for d in (1, -1):
                send(("q2", a, 0, d), piece(a, 0, 0), piece(a, 0, 0), turn(a, 1, d))
        arrive("y_up", grow_ref.at[line_at(c_of(-1))], chip(dy=-1))
        arrive("y_down", grow_ref.at[line_at(c_of(1))], chip(dy=1))
        send("y_far_up", grow_ref.at[line_at(c_of(-1), 0, h)], grow_ref.at[line_at(c_of(-1), 0, h)], chip(dy=1))
        send("y_far_down", grow_ref.at[line_at(c_of(1), h, h)], grow_ref.at[line_at(c_of(1), h, h)], chip(dy=-1))
        for d in (-1, 1):
            send(("c", d), grow_ref.at[line_at(c_of(d))], grow_ref.at[line_at(c_of(d))], partner)

    def p2():
        for a in (0, 1):
            for d in (1, -1):
                arrive(("q1", a, d), piece(a, -d, 0), turn(a, 0, -d))
                lo = 0 if d == 1 else h // 2
                send(("q1r", a, d), piece(a, -d, 0, lo, h // 2), piece(a, -d, 0, lo, h // 2), turn(a, 0, d))
        for a in (0, 1):
            for k in (-1, 1):
                for d in (1, -1):
                    send(("q2", a, k, d), piece(a, k, 0), piece(a, k, 0), turn(a, 1, d))

    def p3():
        for a in (0, 1):
            for d in (1, -1):
                lo = 0 if d == 1 else h // 2
                arrive(("q1r", a, d), piece(a, -2 * d, 0, lo, h // 2), turn(a, 0, -d))
            for d in (1, -1):
                send(("q2", a, 2, d), piece(a, 2, 0), piece(a, 2, 0), turn(a, 1, d))

    def relay(a, k, d):
        arrive(("q2", a, k, d), piece(a, k, -d), turn(a, 1, -d))
        if (k in (0, -1)) == (d == 1):
            send(("q2r", a, k), piece(a, k, -d), piece(a, k, -d), turn(a, 1, d))

    def relays(*ks):
        def run():
            for k in ks:
                for a in (0, 1):
                    for d in (1, -1):
                        relay(a, k, d)
        return run

    def p4():
        arrive("y_far_up", grow_ref.at[line_at(c_of(-2), 0, h)], chip(dy=-1))
        arrive("y_far_down", grow_ref.at[line_at(c_of(2), h, h)], chip(dy=1))
        send(("c", 2), grow_ref.at[line_at(c_of(2))], grow_ref.at[line_at(c_of(2))], partner)

    def edge_lines():
        for key, _, dst, _, frm in halo[2:] + sum(strips, []):
            arrive(key, dst, frm)
        forecast_lines(0, 1)
        forecast_lines(lines - 1, lines)

    hooks = {(1, 2): [p1], (2, 1): [p2], (3, 0): [p3, relays(0)], (3, 3): [p4, relays(-1)], (4, 0): [edge_lines, relays(1, 2)]}

    arrive("s_back", s_out.at[pl.ds(other, half), :], partner)
    invert_in(s_out, noise_ref, sinv_ref, hooks)

    for d in (0, -1, 1, 2):
        there = line_at(2 * step(y, d) + 1 - core)
        arrive(("c", d), grow_ref.at[there], partner)

    def update_rows(n, _):
        at = pl.ds(pl.multiple_of(n * 2 * cells, 2 * cells), 2 * cells)
        w = jnp.dot(grow_ref[at, :], sinv_ref[...], precision=HI, preferred_element_type=F32)
        wh_ref[at, :], wlo_ref[at, :] = split(w)
        return 0
    lax.fori_loop(0, lines // 2, update_rows, 0)
    for a in (0, 1):
        for k in (0, -1, 1, 2):
            d = 1 if k in (0, -1) else -1
            arrive(("q2r", a, k), piece(a, k, -2 * d), turn(a, 1, -d))
    for c in sent:
        c.wait_send()
    for n in range(lines):
        pltpu.make_async_copy(f_ref.at[n], f_hbm.at[n], out_sems.at[n]).wait()

    @pl.when(jnp.logical_not(alone))
    def _():
        twin_copy.wait_send()


def exchange(p, velf, vels, obs, noise):
    rows, cols = p.shape
    count, cells = obs.shape[1], velf.shape[0]
    lines = rows // cells
    half = count // 2
    p1, p2 = half // RING, half // RING**2
    v = pl.BlockSpec(memory_space=pltpu.VMEM)
    hbm = pl.BlockSpec(memory_space=pl.ANY)
    shape = lambda *s: jax.ShapeDtypeStruct(s, F32)
    vmem = lambda *s: pltpu.VMEM(s, F32)
    return pl.pallas_call(exchange_kernel,
        out_shape=(jax.ShapeDtypeStruct((rows, count), BF16), jax.ShapeDtypeStruct((rows, count), BF16), shape(cols, count),
                   shape(lines, cells, cols)),
        in_specs=[hbm, v, v, v, v],
        out_specs=(v, v, hbm, hbm),
        scratch_shapes=[
            vmem(lines + 2, cells, cols + 2 * cells), pltpu.VMEM((cols, count), BF16), pltpu.VMEM((cols, count), BF16),
            vmem(16, count), vmem(lines, 4, cells, cells), vmem(cols // cells, 8, cells), vmem(cols // cells + 2, cells, cells),
            vmem(lines, cells, cols), vmem(lines + 2, cells, count), vmem(count, count),
            vmem(lines, cells, count), vmem(RING, cells, count), vmem(RING, cells, count),
            vmem(2, cells // 2, count), vmem(2, cells, count),
            vmem(count, count), vmem(half, count), vmem(2, 3, p1, half), vmem(2, 3, p2, half), vmem(2, RING, p2, half),
            vmem(count, count), vmem(count, count), vmem(rows, count),
            pltpu.SemaphoreType.DMA((lines,)), pltpu.SemaphoreType.DMA((lines,)), pltpu.SemaphoreType.DMA,
            pltpu.SemaphoreType.DMA((100,)), pltpu.SemaphoreType.DMA((100,))],
        compiler_params=pltpu.CompilerParams(vmem_limit_bytes=62 << 20, collective_id=0, has_side_effects=True),
        cost_estimate=pl.CostEstimate(flops=12 * 10**9, bytes_accessed=28 << 20, transcendentals=0),
    )(p.reshape(lines, cells, cols), velf, vels, obs, noise)


def body(prior, vel_first, vel_second, obs_cell, obs_noise):
    w_high, w_low, g_cols, field = exchange(prior, vel_first, vel_second, obs_cell.T, obs_noise[None])
    return finish(field.reshape(prior.shape), w_high, w_low, g_cols)


def solution(mesh):
    placed = (P("row", "col"), P(), P(), P(), P())
    return jax.shard_map(body, mesh=mesh, in_specs=placed, out_specs=P("row", "col"), check_vma=False)
```

```python
import functools
import jax
import jax.numpy as jnp
from jax import lax
from jax.experimental import pallas as pl
from jax.experimental.pallas import tpu as pltpu
from jax.sharding import PartitionSpec as P

HI = lax.Precision.HIGHEST
F32, BF16 = jnp.float32, jnp.bfloat16
dispersion = 0.125
centre_weight = 1.0 - 4.0 * dispersion
interp_weights = (0.42, 0.28, 0.18, 0.12)

def split(x):
    hi = x.astype(BF16)
    return hi, (x - hi.astype(F32)).astype(BF16)

def dot3(a, b, dims):
    (ah, al), (bh, bl) = a, b
    dg = functools.partial(lax.dot_general, dimension_numbers=(dims, ((), ())), preferred_element_type=F32)
    return dg(ah, bh) + (dg(ah, bl) + dg(al, bh))

def observed_weights(velf_ref, vels_ref, oi, oj):
    cells, count = velf_ref.shape[0], oi.shape[1]
    cid = lax.broadcasted_iota(jnp.int32, (cells, count), 0)
    w = {}
    def add(di, dj, v):
        w[di, dj] = w[di, dj] + v if (di, dj) in w else v
    for a in (0, 1):
        pick = jnp.where(cid == oi + a, 1.0, 0.0).astype(F32)
        by_j = [lax.dot_general(v[...], pick, (((0,), (0,)), ((), ())), precision=HI, preferred_element_type=F32)
                for v in (velf_ref, vels_ref)]
        for b in (0, 1):
            here = cid == oj + b
            vf, vs = [jnp.sum(jnp.where(here, x, 0.0), axis=0, keepdims=True) for x in by_j]
            h = interp_weights[2 * a + b]
            add(a, b, jnp.full_like(vf, h * centre_weight))
            add(a + 1, b, h * (dispersion - 0.5 * vf))
            add(a - 1, b, h * (dispersion + 0.5 * vf))
            add(a, b + 1, h * (dispersion - 0.5 * vs))
            add(a, b - 1, h * (dispersion + 0.5 * vs))
    return w

def line_weights(w, oi, oj, line, cells):
    count = oi.shape[1]
    jid = lax.broadcasted_iota(jnp.int32, (cells, count), 0)
    out = jnp.zeros((cells, count), F32)
    for dj in (-1, 0, 1, 2):
        row = jnp.zeros((1, count), F32)
        for di in (-1, 0, 1, 2):
            if (di, dj) in w:
                row = row + jnp.where(oi + di == line, w[di, dj], 0.0)
        out = jnp.where(jid == oj + dj, row, out)
    return out


def observed_panel(first_row, first_col, fetch, velf_ref, vels_ref, obs_ref, ext, t_ext, s_ref, ch, cl, wsc, send_edges):
    cells = velf_ref.shape[0]
    lines, cols = ext.shape[0] - 2, ext.shape[2] - 2 * cells
    w = observed_weights(velf_ref, vels_ref, obs_ref[0:1, :], obs_ref[1:2, :])
    keys = sorted(w)
    for n, key in enumerate(keys):
        wsc[n:n + 1, :] = w[key]

    def at_line(line):
        table = {key: wsc[n:n + 1, :] for n, key in enumerate(keys)}
        return line_weights(table, obs_ref[0:1, :], obs_ref[1:2, :], line, cells)

    def build(l, _):
        at = pl.ds(pl.multiple_of(l * cells, cells), cells)
        ch[at, :], cl[at, :] = split(at_line(first_col + l))
        return 0
    lax.fori_loop(0, cols // cells, build, 0)
    s_ref[...] = jnp.zeros_like(s_ref)
    take = 2

    def run(n, _):
        for m in range(take):
            fetch(n * take + m).wait()
        at = pl.ds(1 + n * take, take)
        p = ext[at, :, cells:cells + cols].reshape(take * cells, cols)
        t = dot3(split(p), (ch[...], cl[...]), ((1,), (0,)))
        t_ext[at] = t.reshape(take, cells, t.shape[1])
        c = jnp.concatenate([at_line(first_row + n * take + m) for m in range(take)], axis=0)
        s_ref[...] += dot3(split(c), split(t), ((0,), (0,)))
        return 0
    last = lines // take - 1
    lax.fori_loop(0, 2, lambda n, _: run(n * last, _), 0)
    send_edges()
    lax.fori_loop(1, last, run, 0)


def left_sweep(prev, mid, nxt, w):
    cells = mid.shape[0]
    up = pltpu.roll(mid, cells - 1, 0)
    down = pltpu.roll(mid, 1, 0)
    return centre_weight * mid + w[0] * nxt + w[1] * prev + w[2] * up + w[3] * down


def stencil_tables(velf_ref, vels_ref, first_row, first_col, wl, wr):
    cells = velf_ref.shape[0]
    by_first, by_second = velf_ref[...].T, vels_ref[...].T
    rid = lax.broadcasted_iota(jnp.int32, (cells, cells), 0)
    cid = lax.broadcasted_iota(jnp.int32, (cells, cells), 1)
    ends = cells - 1

    def row_line(l, _):
        line = first_row + l
        here = cid == line
        a, b = [jnp.broadcast_to(jnp.sum(jnp.where(here, v, 0.0), axis=1, keepdims=True), (cells, cells))
                for v in (by_first, by_second)]
        wl[l, 0] = jnp.where(line == ends, 0.0, dispersion - 0.5 * a)
        wl[l, 1] = jnp.where(line == 0, 0.0, dispersion + 0.5 * a)
        wl[l, 2] = jnp.where(rid == ends, 0.0, dispersion - 0.5 * b)
        wl[l, 3] = jnp.where(rid == 0, 0.0, dispersion + 0.5 * b)
        return 0
    lax.fori_loop(0, wl.shape[0], row_line, 0)

    def col_line(l, _):
        line = first_col + l
        a, b = velf_ref[pl.ds(line, 1), :], vels_ref[pl.ds(line, 1), :]
        lane = cid[:1]
        wr[l, 0:1, :] = jnp.where(line == ends, 0.0, dispersion - 0.5 * a)
        wr[l, 1:2, :] = jnp.where(line == 0, 0.0, dispersion + 0.5 * a)
        wr[l, 2:3, :] = jnp.where(lane == ends, 0.0, dispersion - 0.5 * b)
        wr[l, 3:4, :] = jnp.where(lane == 0, 0.0, dispersion + 0.5 * b)
        return 0
    lax.fori_loop(0, wr.shape[0], col_line, 0)


def forecast_line(i, ext, wl, wr, q_ref, f_ref):
    cells = ext.shape[1]
    spans = q_ref.shape[0]

    def rows_of(l):
        s = pl.ds(pl.multiple_of(l * cells, cells), cells)
        w = [wl[i, m] for m in range(4)]
        q_ref[l] = left_sweep(ext[i, :, s], ext[i + 1, :, s], ext[i + 2, :, s], w)

    def cols_of(l):
        s = pl.ds(pl.multiple_of(l * cells, cells), cells)
        mid = q_ref[l + 1]
        f_ref[i, :, s] = (centre_weight * mid + wr[l, 0:1, :] * q_ref[l + 2] + wr[l, 1:2, :] * q_ref[l]
                          + wr[l, 2:3, :] * pltpu.roll(mid, cells - 1, 1) + wr[l, 3:4, :] * pltpu.roll(mid, 1, 1))

    def pair(f):
        def run(n, _):
            f(2 * n)
            f(2 * n + 1)
            return 0
        return run
    lax.fori_loop(0, spans // 2, pair(rows_of), 0)
    lax.fori_loop(0, spans // 2 - 1, pair(cols_of), 0)


def fin_kernel(f_ref, wh_ref, wlo_ref, gc_ref, o_ref):
    o_ref[...] = f_ref[...] - dot3((wh_ref[...], wlo_ref[...]), split(gc_ref[...]), ((1,), (1,)))


def finish(f, wh, wlo, gc, tile=512):
    rows, cols = f.shape
    count = gc.shape[1]
    whole = lambda x: pl.BlockSpec(x.shape, lambda n: (0, 0), pipeline_mode=pl.Buffered(1))
    return pl.pallas_call(fin_kernel, grid=(cols // tile,),
        out_shape=jax.ShapeDtypeStruct((rows, cols), F32),
        in_specs=[pl.BlockSpec((rows, tile), lambda n: (0, n)), whole(wh), whole(wlo), pl.BlockSpec((tile, count), lambda n: (n, 0))],
        out_specs=pl.BlockSpec((rows, tile), lambda n: (0, n)),
        compiler_params=pltpu.CompilerParams(vmem_limit_bytes=62 << 20),
        cost_estimate=pl.CostEstimate(flops=8 * 10**9, bytes_accessed=24 << 20, transcendentals=0),
    )(f, wh, wlo, gc)


def invert_in(s_ref, noise_ref, o_ref, hooks, block=128, parts=4):
    n = s_ref.shape[0]
    s = s_ref[...]
    rid = lax.broadcasted_iota(jnp.int32, (n, n), 0)
    cid = lax.broadcasted_iota(jnp.int32, (n, n), 1)
    o_ref[...] = 0.5 * (s + s.T) + jnp.where(rid == cid, noise_ref[...], 0.0)
    nb = n // block
    for k in range(nb):
        own = slice(k * block, (k + 1) * block)
        a = o_ref[own, own]
        for part in range(parts):
            for hook in hooks.get((k, part), ()):
                hook()
            a = pivot(a, range(part * block // parts, (part + 1) * block // parts, 4))
        panel = jnp.dot(a, o_ref[own, :], precision=HI, preferred_element_type=F32)
        col = o_ref[:, own]
        for j in range(nb):
            here = slice(j * block, (j + 1) * block)
            r = a if j == k else panel[:, here]
            upd = jnp.dot(col, r, precision=HI, preferred_element_type=F32)
            o_ref[:, here] = -upd if j == k else o_ref[:, here] - upd
            o_ref[own, here] = r
    for hook in hooks.get((nb, 0), ()):
        hook()


def pivot(a, steps):
    rid = lax.broadcasted_iota(jnp.int32, a.shape, 0)
    cid = lax.broadcasted_iota(jnp.int32, a.shape, 1)
    lane = cid[:1]
    four = range(4)
    for k in steps:
        col = [jnp.broadcast_to(a[:, k + j:k + j + 1], a.shape) for j in four]
        p = {(i, j): col[j][k + i:k + i + 1, :] for j in four for i in range(j + 1)}
        inside = (lane >= k) & (lane < k + 4)
        row = [jnp.where(inside, jnp.where(lane == k + j, 1.0, 0.0), a[k + j:k + j + 1, :]) for j in four]
        det = 1.0 / (p[0, 0] * p[1, 1] - p[0, 1] * p[0, 1])
        a00, a01, a11 = p[1, 1] * det, -p[0, 1] * det, p[0, 0] * det
        x00, x01 = a00 * p[0, 2] + a01 * p[1, 2], a00 * p[0, 3] + a01 * p[1, 3]
        x10, x11 = a01 * p[0, 2] + a11 * p[1, 2], a01 * p[0, 3] + a11 * p[1, 3]
        s22 = p[2, 2] - (p[0, 2] * x00 + p[1, 2] * x10)
        s23 = p[2, 3] - (p[0, 2] * x01 + p[1, 2] * x11)
        s33 = p[3, 3] - (p[0, 3] * x01 + p[1, 3] * x11)
        u0, u1 = a00 * row[0] + a01 * row[1], a01 * row[0] + a11 * row[1]
        v2 = row[2] - (x00 * row[0] + x10 * row[1])
        v3 = row[3] - (x01 * row[0] + x11 * row[1])
        det = 1.0 / (s22 * s33 - s23 * s23)
        r2, r3 = (s33 * v2 - s23 * v3) * det, (s22 * v3 - s23 * v2) * det
        r0, r1 = u0 - (x00 * r2 + x01 * r3), u1 - (x10 * r2 + x11 * r3)
        base = jnp.where((cid >= k) & (cid < k + 4), 0.0, a)
        a = base - ((col[0] * r0 + col[1] * r1) + (col[2] * r2 + col[3] * r3))
        for j, r in enumerate((r0, r1, r2, r3)):
            a = jnp.where(rid == k + j, r, a)
    return a


MESH = pl.DeviceIdType.MESH
RING = 4


def exchange_kernel(p_hbm, velf_ref, vels_ref, obs_ref, noise_ref,
                    wh_ref, wlo_ref, gcol_ref, f_hbm,
                    ext, ch, cl, wsc, wl, wr, q_ref, f_ref, t_ext, s_ref, gp, rg, gs, ry, rl,
                    s_acc, r0, r1, r2, r3, s_out, sinv_ref, grow_ref, in_sems, out_sems, twin_sem, send_sems, recv_sems):
    lines, cells, cols = p_hbm.shape
    count = obs_ref.shape[1]
    row, col = lax.axis_index("row"), lax.axis_index("col")
    row_count, col_count = lax.axis_size("row"), lax.axis_size("col")
    x, z = row // RING, row % RING
    y, core = col // 2, col % 2
    col_lines = cols // cells
    inner = pl.ds(cells, cols)

    def fetch(n):
        return pltpu.make_async_copy(p_hbm.at[n], ext.at[n + 1, :, inner], in_sems.at[n])

    for n in range(lines):
        fetch(n).start()

    def step(v, d):
        return (v + d + RING) % RING

    def chip(dx=0, dy=0, dz=0):
        return (step(x, dx) * RING + step(z, dz), step(y, dy) * 2 + core)

    partner = (row, col + 1 - 2 * core)
    twin_row = y * RING + 2 * core + z % 2
    twin_col = 2 * x + z // 2
    twin = (twin_row, twin_col)
    alone = (twin_row == row) & (twin_col == col)
    up, down = (row + 1) % row_count, (row + row_count - 1) % row_count
    right, left = (col + 1) % col_count, (col + col_count - 1) % col_count

    barrier = pltpu.get_barrier_semaphore()
    greeted = [partner, (up, col), (down, col), (row, right), (row, left),
               (up, right), (up, left), (down, right), (down, left)]
    greeted += [chip(dx=d) for d in (1, 2, 3)] + [chip(dy=d) for d in (1, 2, 3)] + [chip(dz=d) for d in (1, 2, 3)]
    for peer in greeted:
        pl.semaphore_signal(barrier, inc=1, device_id=peer, device_id_type=MESH)

    @pl.when(jnp.logical_not(alone))
    def _():
        pl.semaphore_signal(barrier, inc=1, device_id=twin, device_id_type=MESH)
    pl.semaphore_wait(barrier, len(greeted) + 1 - alone.astype(jnp.int32))

    used, sent = {}, []

    def slot(key):
        if key not in used:
            used[key] = len(used)
        return used[key]

    def copy(key, src, dst, peer):
        n = slot(key)
        return pltpu.make_async_remote_copy(src_ref=src, dst_ref=dst, send_sem=send_sems.at[n], recv_sem=recv_sems.at[n],
                                            device_id=peer, device_id_type=MESH)

    def send(key, src, dst, peer):
        c = copy(key, src, dst, peer)
        c.start()
        sent.append(c)

    def arrive(key, dst, peer):
        copy(key, dst, dst, peer).wait_recv()

    low, high = pl.ds(0, cells), pl.ds(cols + cells, cells)
    head, tail = pl.ds(0, cells), pl.ds(cols - cells, cells)
    top, bot = 0, lines + 1
    bounds = [cols * n // 16 for n in (0, 6, 8, 9, 10, 16)]
    block = pl.ds(1, lines)
    halo = [
        ("p_right", p_hbm.at[:, :, tail], ext.at[block, :, low], (row, right), (row, left)),
        ("p_left", p_hbm.at[:, :, head], ext.at[block, :, high], (row, left), (row, right)),
        ("p_up_right", p_hbm.at[lines - 1, :, tail], ext.at[top, :, low], (up, right), (down, left)),
        ("p_up_left", p_hbm.at[lines - 1, :, head], ext.at[top, :, high], (up, left), (down, right)),
        ("p_down_right", p_hbm.at[0, :, tail], ext.at[bot, :, low], (down, right), (up, left)),
        ("p_down_left", p_hbm.at[0, :, head], ext.at[bot, :, high], (down, left), (up, right)),
    ]
    strips = []
    for n, (lo, hi) in enumerate(zip(bounds[:-1], bounds[1:])):
        src, dst = pl.ds(lo, hi - lo), pl.ds(cells + lo, hi - lo)
        strips.append([
            (("p_up", n), p_hbm.at[lines - 1, :, src], ext.at[top, :, dst], (up, col), (down, col)),
            (("p_down", n), p_hbm.at[0, :, src], ext.at[bot, :, dst], (down, col), (up, col))])

    def send_strip(n):
        for key, src, dst, to, _ in strips[n]:
            send(key, src, dst, to)

    for key, src, dst, to, _ in halo:
        send(key, src, dst, to)
    send_strip(0)

    first_row, first_col = row * lines, col * col_lines
    stencil_tables(velf_ref, vels_ref, first_row, first_col, wl, wr)
    def send_edges():
        send("t_up", t_ext.at[lines], t_ext.at[top], (up, col))
        send("t_down", t_ext.at[1], t_ext.at[bot], (down, col))

    observed_panel(first_row, first_col, fetch, velf_ref, vels_ref, obs_ref, ext, t_ext, s_ref, ch, cl, wsc, send_edges)

    def forecast_lines(start, stop):
        def one(i, _):
            forecast_line(i, ext, wl, wr, q_ref, f_ref)
            pltpu.make_async_copy(f_ref.at[i], f_hbm.at[i], out_sems.at[i]).start()
            return 0
        lax.fori_loop(start, stop, one, 0)

    half = count // 2
    mine = pl.multiple_of(core * half, half)
    other = pl.multiple_of(half - core * half, half)
    send("s_core", s_ref.at[pl.ds(other, half), :], r0.at[:, :], partner)
    for key, _, dst, _, frm in halo[:2]:
        arrive(key, dst, frm)
    forecast_lines(1, 2)
    arrive("s_core", r0.at[:, :], partner)
    s_acc[pl.ds(mine, half), :] = s_ref[pl.ds(mine, half), :] + r0[...]

    wide = count // 2
    p1, p2 = half // RING, half // RING**2
    order = (("x", "y"), ("y", "x"))
    pos = {"x": x, "y": y, "z": z}

    def at1(a, i):
        return (pl.ds(pl.multiple_of(mine + i * p1, 8), p1), pl.ds(a * wide, wide))

    def at2(a, i, j):
        return (pl.ds(pl.multiple_of(mine + i * p1 + j * p2, 8), p2), pl.ds(a * wide, wide))

    def hop(axis, d):
        return chip(**{"d" + axis: d})

    def reduce_start(name, slots, place, axes):
        for a in (0, 1):
            for d in (1, 2, 3):
                axis = axes[a]
                send((name, a, d), s_acc.at[place(a, step(pos[axis], d))], slots.at[a, d - 1], hop(axis, d))

    def reduce_end(name, slots, place, axes):
        for a in (0, 1):
            for d in (1, 2, 3):
                arrive((name, a, d), slots.at[a, d - 1], hop(axes[a], -d))
            here = place(a, pos[axes[a]])
            s_acc[here] = (s_acc[here] + slots[a, 0]) + (slots[a, 1] + slots[a, 2])

    def gather_start(name, place, axes):
        for a in (0, 1):
            here = place(a, pos[axes[a]])
            for d in (1, 2, 3):
                send((name, a, d), s_out.at[here], s_out.at[here], hop(axes[a], d))

    def gather_end(name, place, axes):
        for a in (0, 1):
            for d in (1, 2, 3):
                there = place(a, step(pos[axes[a]], -d))
                arrive((name, a, d), s_out.at[there], hop(axes[a], -d))

    axes1, axes2 = [o[0] for o in order], [o[1] for o in order]
    own1 = [pos[a] for a in axes1]
    own2 = [pos[a] for a in axes2]
    place1 = at1
    place2 = lambda a, j: at2(a, own1[a], j)

    reduce_start("s1", r1, place1, axes1)
    send_strip(1)


    arrive("t_up", t_ext.at[top], (down, col))
    arrive("t_down", t_ext.at[bot], (up, col))

    def sweep_line(l, _):
        w = [wl[l, m] for m in range(4)]
        for b in range(count // cells):
            s = slice(b * cells, (b + 1) * cells)
            gp[l, :, s] = left_sweep(t_ext[l, :, s], t_ext[l + 1, :, s], t_ext[l + 2, :, s], w)
        return 0
    lax.fori_loop(0, lines, sweep_line, 0)
    for q in range(RING):
        send(("g_core", q), gp.at[2 * q + 1 - core], rg.at[q], partner)
    forecast_lines(2, 3)

    reduce_end("s1", r1, place1, axes1)
    reduce_start("s2", r2, place2, axes2)
    send_strip(2)

    for q in range(RING):
        arrive(("g_core", q), rg.at[q], partner)
        gs[q] = gp[2 * q + core] + rg[q]
    h = cells // 2
    first, second = pl.ds(0, h), pl.ds(h, h)
    far, nxt_y, prv_y = step(y, 2), step(y, 1), step(y, -1)
    send("g_far_up", gs.at[far, first], ry.at[0], chip(dy=1))
    send("g_far_down", gs.at[far, second], ry.at[1], chip(dy=-1))

    forecast_lines(3, 4)
    reduce_end("s2", r2, place2, axes2)
    for a in (0, 1):
        piece2 = s_acc.at[place2(a, own2[a])]
        for d in (1, 2, 3):
            send(("s3", a, d), piece2, r3.at[a, z], chip(dz=d))
        r3[a, z] = s_acc[place2(a, own2[a])]

    forecast_lines(4, 5)
    for a in (0, 1):
        for d in (1, 2, 3):
            arrive(("s3", a, d), r3.at[a, step(z, -d)], chip(dz=-d))
        s_out[place2(a, own2[a])] = (r3[a, 0] + r3[a, 1]) + (r3[a, 2] + r3[a, 3])
    gather_start("a2", place2, axes2)
    arrive("g_far_up", ry.at[0], chip(dy=-1))
    arrive("g_far_down", ry.at[1], chip(dy=1))
    gs[nxt_y, first] = gs[nxt_y, first] + ry[0]
    gs[prv_y, second] = gs[prv_y, second] + ry[1]
    send("g_up", gs.at[nxt_y], rl.at[0], chip(dy=1))
    send("g_down", gs.at[prv_y], rl.at[1], chip(dy=-1))
    send_strip(3)
    forecast_lines(5, 6)
    gather_end("a2", place2, axes2)
    gather_start("a1", place1, axes1)
    send_strip(4)
    forecast_lines(6, 7)

    arrive("g_up", rl.at[0], chip(dy=-1))
    arrive("g_down", rl.at[1], chip(dy=1))

    def line_at(c, lo=0, n=cells):
        return (pl.ds(pl.multiple_of(c * cells + lo, 8), n), slice(None))

    own = line_at(col)
    grow_ref[own] = (gs[y] + rl[0]) + rl[1]

    def col_line(xx, zz, lo=0, n=cells):
        return line_at(8 * (zz % 2) + 2 * xx + zz // 2, lo, n)

    landing = col_line(x, z)
    away = line_at(8 * (row % 2) + col)
    twin_copy = copy("twin", grow_ref.at[own], gcol_ref.at[away], twin)

    @pl.when(alone)
    def _():
        pltpu.make_async_copy(grow_ref.at[own], gcol_ref.at[landing], twin_sem).start()

    @pl.when(jnp.logical_not(alone))
    def _():
        twin_copy.start()

    send("y_up", grow_ref.at[own], grow_ref.at[own], chip(dy=1))
    send("y_down", grow_ref.at[own], grow_ref.at[own], chip(dy=-1))
    send(("c", 0), grow_ref.at[own], grow_ref.at[own], partner)

    gather_end("a1", place1, axes1)
    whole = (pl.ds(mine, half), slice(None))
    send("s_back", s_out.at[whole], s_out.at[whole], partner)

    def c_of(d):
        return 2 * step(y, d) + core

    def twin_landed():
        @pl.when(jnp.logical_not(alone))
        def _():
            arrive("twin", gcol_ref.at[landing], twin)

        @pl.when(alone)
        def _():
            pltpu.make_async_copy(grow_ref.at[own], gcol_ref.at[landing], twin_sem).wait()

    lows = (0, h)
    rings = (("x", "z"), ("z", "x"))

    def piece(a, d0, d1, lo=0, n=h):
        dx, dz = (d0, d1) if a == 0 else (d1, d0)
        return gcol_ref.at[col_line(step(x, dx), step(z, dz), lows[a] + lo, n)]

    def turn(a, level, d):
        return hop(rings[a][level], d)

    def p1():
        twin_landed()
        for a in (0, 1):
            for d in (1, -1):
                send(("q1", a, d), piece(a, 0, 0), piece(a, 0, 0), turn(a, 0, d))
        for a in (0, 1):
            for d in (1, -1):
                send(("q2", a, 0, d), piece(a, 0, 0), piece(a, 0, 0), turn(a, 1, d))
        arrive("y_up", grow_ref.at[line_at(c_of(-1))], chip(dy=-1))
        arrive("y_down", grow_ref.at[line_at(c_of(1))], chip(dy=1))
        send("y_far_up", grow_ref.at[line_at(c_of(-1), 0, h)], grow_ref.at[line_at(c_of(-1), 0, h)], chip(dy=1))
        send("y_far_down", grow_ref.at[line_at(c_of(1), h, h)], grow_ref.at[line_at(c_of(1), h, h)], chip(dy=-1))
        for d in (-1, 1):
            send(("c", d), grow_ref.at[line_at(c_of(d))], grow_ref.at[line_at(c_of(d))], partner)

    def p2():
        for a in (0, 1):
            for d in (1, -1):
                arrive(("q1", a, d), piece(a, -d, 0), turn(a, 0, -d))
                lo = 0 if d == 1 else h // 2
                send(("q1r", a, d), piece(a, -d, 0, lo, h // 2), piece(a, -d, 0, lo, h // 2), turn(a, 0, d))
        for a in (0, 1):
            for k in (-1, 1):
                for d in (1, -1):
                    send(("q2", a, k, d), piece(a, k, 0), piece(a, k, 0), turn(a, 1, d))

    def p3():
        for a in (0, 1):
            for d in (1, -1):
                lo = 0 if d == 1 else h // 2
                arrive(("q1r", a, d), piece(a, -2 * d, 0, lo, h // 2), turn(a, 0, -d))
            for d in (1, -1):
                send(("q2", a, 2, d), piece(a, 2, 0), piece(a, 2, 0), turn(a, 1, d))

    def relay(a, k, d):
        arrive(("q2", a, k, d), piece(a, k, -d), turn(a, 1, -d))
        if (k in (0, -1)) == (d == 1):
            send(("q2r", a, k), piece(a, k, -d), piece(a, k, -d), turn(a, 1, d))

    def relays(*ks):
        def run():
            for k in ks:
                for a in (0, 1):
                    for d in (1, -1):
                        relay(a, k, d)
        return run

    def p4():
        arrive("y_far_up", grow_ref.at[line_at(c_of(-2), 0, h)], chip(dy=-1))
        arrive("y_far_down", grow_ref.at[line_at(c_of(2), h, h)], chip(dy=1))
        send(("c", 2), grow_ref.at[line_at(c_of(2))], grow_ref.at[line_at(c_of(2))], partner)

    def edge_lines():
        for key, _, dst, _, frm in halo[2:] + sum(strips, []):
            arrive(key, dst, frm)
        forecast_lines(0, 1)
        forecast_lines(lines - 1, lines)

    hooks = {(1, 2): [p1], (2, 1): [p2], (3, 0): [p3, relays(0)], (3, 3): [p4, relays(-1)],
             (4, 0): [relays(1), edge_lines, relays(2)]}

    arrive("s_back", s_out.at[pl.ds(other, half), :], partner)
    invert_in(s_out, noise_ref, sinv_ref, hooks)

    for d in (0, -1, 1, 2):
        there = line_at(2 * step(y, d) + 1 - core)
        arrive(("c", d), grow_ref.at[there], partner)

    def update_rows(n, _):
        at = pl.ds(pl.multiple_of(n * 2 * cells, 2 * cells), 2 * cells)
        w = jnp.dot(grow_ref[at, :], sinv_ref[...], precision=HI, preferred_element_type=F32)
        wh_ref[at, :], wlo_ref[at, :] = split(w)
        return 0
    lax.fori_loop(0, lines // 2, update_rows, 0)
    for a in (0, 1):
        for k in (0, -1, 1, 2):
            d = 1 if k in (0, -1) else -1
            arrive(("q2r", a, k), piece(a, k, -2 * d), turn(a, 1, -d))
    for c in sent:
        c.wait_send()
    for n in range(lines):
        pltpu.make_async_copy(f_ref.at[n], f_hbm.at[n], out_sems.at[n]).wait()

    @pl.when(jnp.logical_not(alone))
    def _():
        twin_copy.wait_send()


def exchange(p, velf, vels, obs, noise):
    rows, cols = p.shape
    count, cells = obs.shape[1], velf.shape[0]
    lines = rows // cells
    half = count // 2
    p1, p2 = half // RING, half // RING**2
    v = pl.BlockSpec(memory_space=pltpu.VMEM)
    hbm = pl.BlockSpec(memory_space=pl.ANY)
    shape = lambda *s: jax.ShapeDtypeStruct(s, F32)
    vmem = lambda *s: pltpu.VMEM(s, F32)
    return pl.pallas_call(exchange_kernel,
        out_shape=(jax.ShapeDtypeStruct((rows, count), BF16), jax.ShapeDtypeStruct((rows, count), BF16), shape(cols, count),
                   shape(lines, cells, cols)),
        in_specs=[hbm, v, v, v, v],
        out_specs=(v, v, hbm, hbm),
        scratch_shapes=[
            vmem(lines + 2, cells, cols + 2 * cells), pltpu.VMEM((cols, count), BF16), pltpu.VMEM((cols, count), BF16),
            vmem(16, count), vmem(lines, 4, cells, cells), vmem(cols // cells, 8, cells), vmem(cols // cells + 2, cells, cells),
            vmem(lines, cells, cols), vmem(lines + 2, cells, count), vmem(count, count),
            vmem(lines, cells, count), vmem(RING, cells, count), vmem(RING, cells, count),
            vmem(2, cells // 2, count), vmem(2, cells, count),
            vmem(count, count), vmem(half, count), vmem(2, 3, p1, half), vmem(2, 3, p2, half), vmem(2, RING, p2, half),
            vmem(count, count), vmem(count, count), vmem(rows, count),
            pltpu.SemaphoreType.DMA((lines,)), pltpu.SemaphoreType.DMA((lines,)), pltpu.SemaphoreType.DMA,
            pltpu.SemaphoreType.DMA((100,)), pltpu.SemaphoreType.DMA((100,))],
        compiler_params=pltpu.CompilerParams(vmem_limit_bytes=62 << 20, collective_id=0, has_side_effects=True),
        cost_estimate=pl.CostEstimate(flops=12 * 10**9, bytes_accessed=28 << 20, transcendentals=0),
    )(p.reshape(lines, cells, cols), velf, vels, obs, noise)


def body(prior, vel_first, vel_second, obs_cell, obs_noise):
    w_high, w_low, g_cols, field = exchange(prior, vel_first, vel_second, obs_cell.T, obs_noise[None])
    return finish(field.reshape(prior.shape), w_high, w_low, g_cols)


def solution(mesh):
    placed = (P("row", "col"), P(), P(), P(), P())
    return jax.shard_map(body, mesh=mesh, in_specs=placed, out_specs=P("row", "col"), check_vma=False)
```
